32 devices in a mesh: expert: 8 (over z, y), tensor: 4 (over x, core).
Axes of the slice: x: 2, y: 2, z: 4, core: 2. Of those that a mesh axis runs over, the one named last changes fastest.
Arguments:
- block_input: bfloat16 [2, 4096, 768], P(None, 'expert', 'tensor')
- norm1_gain: float32 [768], P('tensor'), may hold values from 0.1 to 1.9
- qkv_weight: bfloat16 [3, 768, 768], P(None, None, 'tensor'), may hold values from -0.21875 to 0.21875
- out_weight: bfloat16 [768, 768], P('tensor'), may hold values from -2.5 to 2.5
- pos_table: float32 [32, 12], P(None, 'tensor'), may hold values from -4 to 4
- norm2_gain: float32 [768], P('tensor'), may hold values from 0.1 to 1.9
- expert_in: bfloat16 [8, 768, 3072], P('expert', None, 'tensor'), may hold values from -0.21875 to 0.21875
- expert_down: bfloat16 [8, 3072, 768], P('expert', 'tensor'), may hold values from -0.109375 to 0.109375
- lengths: int32 [2, 8], P(None, 'expert'), may hold values from 128 to 512, as said below
- routes: int32 [2, 4096, 2], P(None, 'expert'), may hold values from 0 to 7, all different within a row; in each aligned block of 512 rows (0 to 511, 512 to 1023, ..., all dimensions but the last counted through in order) at most 160 rows name the same one
- gate_weights: float32 [2, 4096, 2], P(None, 'expert'), may hold values from 0.1 to 1
- output_grad: bfloat16 [2, 4096, 768], P(None, 'expert', 'tensor'), may hold values from -6 to 6
Outputs:
- block_output: float32 [2, 4096, 768], P(None, 'expert', 'tensor')
- input_grad: float32 [2, 4096, 768], P(None, 'expert', 'tensor')
- norm1_gain_grad: float32 [768], P('tensor')
- qkv_weight_grad: float32 [3, 768, 768], P(None, None, 'tensor')
- out_weight_grad: float32 [768, 768], P('tensor')
- pos_table_grad: float32 [32, 12], P(None, 'tensor')
- norm2_gain_grad: float32 [768], P('tensor')
- expert_in_grad: float32 [8, 768, 3072], P('expert', None, 'tensor')
- expert_down_grad: float32 [8, 3072, 768], P('expert', 'tensor')
The draws below stay inside these ranges and needn't reach their ends.
Inputs may be any that keep to these rules, and one draw needn't show every extreme that they name: `routes`: in each micro-batch, the 512 token slots of one sequence name any one expert at most 160 times. `lengths`: every micro-batch holds a sequence that uses all 512 slots.
All inputs are finite; a program needn't handle non-finite values.
Results may differ from the reference program's by a relative error of at most 0.0091.
Values may be sent and summed in bfloat16 or wider, within the bound.
No kernel may reach another device: no remote copies, remote signals or barrier semaphores. Data moves between devices by JAX's collectives and lax.ppermute only.
A program may use at most 192 MiB of HBM per device.

```python
import math
import jax
import jax.numpy as jnp
import numpy as np
from jax import lax

D = 768
HEADS = 12
HD = 64
FF = 3072
TOP = 2
BUCKETS = 32
MAX_DIST = 128
MICRO = 2
SLOT = 512
EXPERTS = 8
TOKENS = 4096
CAP = 160
N_EXPERT = 8


def draw_block_input(key, part):
    noise_key, column_key, row_key = jax.random.split(key, 3)
    column_ids = jnp.arange(D).astype(jnp.float32)
    column_scale = jnp.exp(0.75 * (column_ids / D - 0.5) + jax.random.uniform(column_key, (D,), jnp.float32, -0.6, 0.6))
    noise = jax.random.normal(noise_key, (MICRO, TOKENS, D), jnp.float32)
    row_scale = jnp.exp(jax.random.uniform(row_key, (MICRO, TOKENS, 1), jnp.float32, math.log(0.4), math.log(4.0)))
    return (noise * row_scale * column_scale).astype(jnp.bfloat16)


def draw_lengths(key, part):
    seq_count = TOKENS // SLOT
    length_key, pick_key = jax.random.split(key)
    drawn = jax.random.randint(length_key, (MICRO, seq_count), SLOT // 4, SLOT + 1, jnp.int32)
    full_at = jax.random.randint(pick_key, (MICRO, 1), 0, seq_count, jnp.int32)
    return jnp.where(jnp.arange(seq_count)[None, :] == full_at, SLOT, drawn).astype(jnp.int32)


def levels(own_key, shape, cuts, low, top_value):
    factor_of, own = 1.0, jax.random.fold_in(own_key, 6)
    for dim, parts in cuts:
        heights = jnp.exp(jax.random.uniform(jax.random.fold_in(own, dim), (parts,), jnp.float32, low / len(cuts), top_value / len(cuts)))
        factor_of = factor_of * jnp.repeat(heights, shape[dim] // parts).reshape([-1 if axis == dim else 1 for axis in range(len(shape))])
    return factor_of


def routed_block(stream_key, own, number, rows, number_of, top, limit, lean):
    order = jax.random.permutation(stream_key, number_of)
    crowded, common = portions_of(number_of, rows * top, limit, lean, True), portions_of(number_of, rows * top, limit, lean, False)
    places = jnp.arange(number_of)

    def named(sizes, offset_by):
        used = int((sizes > 0).sum())
        fixed = max(1, used // 4)
        moved = fixed + (places - fixed + offset_by * (used - fixed)) % max(1, number_of - fixed)
        return jnp.zeros((number_of,), jnp.int32).at[order[jnp.where(places < fixed, places, moved)]].set(jnp.asarray(sizes, jnp.int32))

    sizes = jnp.where(number % 4 == 0, named(crowded, number // 4), named(common, number - number // 4 - 1))
    mixed = jax.random.permutation(jax.random.fold_in(own, 3), number_of)
    donor, taker = mixed[0:number_of // 2 * 2:2], mixed[1:number_of // 2 * 2:2]
    margin = jnp.minimum(sizes[donor] - 1, limit - sizes[taker]) // 2
    margin = jnp.where((donor == order[0]) | (taker == order[0]) | (sizes[taker] == 0), 0, jnp.maximum(margin, 0))
    moved = jax.random.randint(jax.random.fold_in(own, 4), (number_of // 2,), 0, 1 << 20) % (margin + 1)
    sizes = sizes.at[donor].add(-moved).at[taker].add(moved)
    members = jnp.searchsorted(jnp.cumsum(sizes), jnp.arange(rows * top), side="right").astype(jnp.int32)
    grid = members.reshape(top, rows).T
    grid = grid[jax.random.permutation(jax.random.fold_in(own, 1), rows)]
    offset_by = jax.random.randint(jax.random.fold_in(own, 2), (rows, 1), 0, top)
    return jnp.take_along_axis(grid, (jnp.arange(top)[None, :] + offset_by) % top, axis=1)


def portions_of(number_of, total, limit, lean, full):
    weights = [(1 << 20) // math.isqrt(standing ** lean) + 1 for standing in range(1, number_of + 1)]
    largest = limit if full else min(limit, max(-(-total // number_of), total * weights[0] // sum(weights)))
    least = 1 if total - largest >= number_of - 1 else 0
    given, rest = [largest] + [least] * (number_of - 1), total - largest - least * (number_of - 1)
    while rest > 0:
        movable = [i for i in range(1, number_of) if given[i] < largest] or [i for i in range(1, number_of) if given[i] < limit]
        mass, left = sum([weights[i] for i in movable]), rest
        for i in movable:
            extra = min(limit - given[i], max(1, left * weights[i] // mass), rest)
            given[i] = given[i] + extra
            rest = rest - extra
    return np.array(given)


def bell_draw(key, dims, width, reach, cuts=(), held_as=jnp.bfloat16):
    gain = levels(key, dims, cuts, -0.22, 0.18) if cuts else 1.0
    values = jax.random.normal(key, dims, jnp.float32) * width * gain
    return jnp.minimum(jnp.maximum(values, -reach), reach).astype(held_as)


def setup_inputs(seed: int = 0) -> dict:
    splits = jax.random.split(jax.random.key(seed), 13)
    block_input = draw_block_input(jax.random.fold_in(splits[12], 71), 0)
    norm1_gain = jnp.clip(1.0 + 0.18 * jax.random.normal(splits[1], (D,), jnp.float32), 0.1, 1.9)
    qkv_weight = bell_draw(splits[2], (3, D, HEADS * HD), D ** -0.5, 0.21875, ((2, 4),))
    out_weight = bell_draw(splits[3], (HEADS * HD, D), (max(HEADS * HD // 128, 1)) ** -0.5, 2.5, ((0, 4),))
    pos_table = bell_draw(splits[4], (BUCKETS, HEADS), 1.0, 4.0, ((1, 4),), jnp.float32)
    norm2_gain = jnp.clip(1.0 + 0.18 * jax.random.normal(splits[5], (D,), jnp.float32), 0.1, 1.9)
    expert_in = bell_draw(splits[6], (EXPERTS, D, FF), D ** -0.5, 0.21875, ((0, 8), (2, 4)))
    expert_down = bell_draw(splits[7], (EXPERTS, FF, D), FF ** -0.5, 0.109375, ((0, 8), (1, 4)))
    lengths = draw_lengths(jax.random.fold_in(splits[12], 71), 0)
    routes_keys = jax.random.split(jax.random.fold_in(splits[9], 1), MICRO * TOKENS // SLOT)
    routes_turns = jax.random.permutation(jax.random.fold_in(splits[9], 3), MICRO * TOKENS // SLOT)
    routes = jax.vmap(lambda own, number: routed_block(jax.random.fold_in(splits[9], 2), own, number, SLOT, EXPERTS, TOP, CAP, 2))(routes_keys, routes_turns).reshape((MICRO, TOKENS, TOP))
    gate_weights = jnp.clip(0.1 + 0.9 * jax.random.uniform(splits[10], (MICRO, TOKENS, TOP), jnp.float32) ** levels(splits[10], (MICRO, TOKENS, TOP), ((1, 8),), -0.2, 0.2), 0.1, 1.0)
    output_grad = bell_draw(splits[11], (MICRO, TOKENS, D), 1.0, 6.0, ((1, 8), (2, 4)))
    return dict(block_input=block_input, norm1_gain=norm1_gain, qkv_weight=qkv_weight, out_weight=out_weight, pos_table=pos_table, norm2_gain=norm2_gain, expert_in=expert_in, expert_down=expert_down, lengths=lengths, routes=routes, gate_weights=gate_weights, output_grad=output_grad)


EPSILON = 1e-06
NEG_LARGE = -1e+30
PRECISE = lax.Precision.HIGHEST

@jax.custom_vjp
def low(v):
    return lax.optimization_barrier(v.astype(jnp.bfloat16)).astype(jnp.float32)

@jax.custom_vjp
def low_back(v):
    return v

def low_keep(v):
    return (low(v), None)

def low_pass(kept, grad):
    return (grad,)

def back_keep(v):
    return (v, None)

def back_low(kept, grad):
    return (low(grad),)
low.defvjp(low_keep, low_pass)
low_back.defvjp(back_keep, back_low)

def bucket_table(position_count, bucket_count, distance_cap):
    distance = np.arange(position_count)
    exact_count = bucket_count // 2
    log_ratio = np.log(np.maximum(distance, 1) / exact_count) / np.log(distance_cap / exact_count)
    spread = exact_count + np.floor(np.maximum(log_ratio, 0.0) * (bucket_count - exact_count)).astype(np.int32)
    spread = np.minimum(spread, bucket_count - 1)
    return np.where(distance < exact_count, distance, spread).astype(np.int32)

def gelu_exact(values):
    return 0.5 * values * (1.0 + lax.erf(values * (1.0 / math.sqrt(2.0))))

def attend_sequence(query_rows, key_rows, value_rows, dist_bias, seq_length):
    block_rows = min(512, SLOT)
    key_ids = jnp.arange(SLOT).astype(jnp.int32)
    score_scale = 1.0 / math.sqrt(HD)

    def one_block(first_row):
        row_ids = first_row + jnp.arange(block_rows).astype(jnp.int32)
        query_block = lax.dynamic_slice_in_dim(query_rows, first_row, block_rows, 0)
        scores = jnp.einsum('qhd,khd->hqk', query_block, key_rows, precision=PRECISE) * score_scale
        offset = jnp.clip(row_ids[:, None] - key_ids[None, :], 0, SLOT - 1)
        scores = low_back(scores + jnp.take(dist_bias, offset, axis=1))
        valid_mask = (key_ids[None, :] <= row_ids[:, None]) & (key_ids[None, :] < seq_length)
        scores = jnp.where(valid_mask[None], scores, NEG_LARGE)
        row_max = lax.optimization_barrier(jnp.max(scores, axis=-1, keepdims=True))
        exp_scores = jnp.exp(scores - row_max)
        attn_probs = low(exp_scores / lax.optimization_barrier(jnp.sum(exp_scores, axis=-1, keepdims=True)))
        return jnp.einsum('hqk,khd->qhd', attn_probs, value_rows, precision=PRECISE)
    starts = (jnp.arange(SLOT // block_rows) * block_rows).astype(jnp.int32)
    block_outs = lax.map(jax.checkpoint(one_block), starts)
    return block_outs.reshape(SLOT, HEADS * HD)

def block_forward(residual_in, norm1_gain, qkv_weight, out_weight, pos_table, norm2_gain, expert_in, expert_down, seq_lengths, route_rows, gate_rows, valid_rows, buckets):
    scale_one = lax.rsqrt(lax.optimization_barrier(jnp.mean(residual_in * residual_in, axis=1, keepdims=True)) + EPSILON)
    normed_one = low(residual_in * scale_one * norm1_gain)
    projected = low(low_back(jnp.einsum('td,cdf->ctf', normed_one, qkv_weight, precision=PRECISE)))
    projected = projected.reshape(3, N_EXPERT, SLOT, HEADS, HD)
    dist_bias = jnp.take(pos_table, buckets, axis=0).T

    def one_sequence(pieces):
        return attend_sequence(pieces[0], pieces[1], pieces[2], dist_bias, pieces[3])
    attended = lax.map(jax.checkpoint(one_sequence), (projected[0], projected[1], projected[2], seq_lengths))
    attended = low(low_back(attended.reshape(TOKENS, HEADS * HD)))
    residual_mid = residual_in + low_back(jnp.dot(attended, out_weight, precision=PRECISE))
    scale_two = lax.rsqrt(lax.optimization_barrier(jnp.mean(residual_mid * residual_mid, axis=1, keepdims=True)) + EPSILON)
    normed_two = low(residual_mid * scale_two * norm2_gain)
    flat_routes = route_rows.reshape(N_EXPERT, SLOT * TOP)
    onehot = (flat_routes[:, :, None] == jnp.arange(EXPERTS).astype(jnp.int32)[None, None, :]).astype(jnp.int32)
    position = lax.optimization_barrier(jnp.sum(jnp.cumsum(onehot, axis=1) * onehot, axis=2)) - 1
    source = jnp.arange(N_EXPERT).astype(jnp.int32)[:, None]
    slot_index = (source * CAP + position).reshape(-1).astype(jnp.int32)
    expert_index = route_rows.reshape(-1).astype(jnp.int32)
    assign_ids = jnp.arange(TOKENS * TOP).astype(jnp.int32)
    slot_owner = jnp.full((EXPERTS, N_EXPERT * CAP), TOKENS * TOP, jnp.int32).at[expert_index, slot_index].set(assign_ids)
    token_of = jnp.where(slot_owner < TOKENS * TOP, slot_owner // TOP, TOKENS).astype(jnp.int32)
    token_table = jnp.concatenate([normed_two, jnp.zeros((1, D), jnp.float32)], axis=0)

    def one_expert(pieces):
        gathered = token_table[pieces[0]]
        pre_act = low_back(jnp.dot(gathered, pieces[1], precision=PRECISE))
        activated = low(gelu_exact(pre_act))
        return low_back(jnp.dot(activated, pieces[2], precision=PRECISE))
    results = lax.map(jax.checkpoint(one_expert), (token_of, expert_in, expert_down))
    picked = results[expert_index, slot_index].reshape(TOKENS, TOP, D)
    gate_mix = gate_rows * valid_rows[:, None]
    moe_out = lax.optimization_barrier(jnp.sum(gate_mix[:, :, None] * picked, axis=1))
    return residual_mid + moe_out

def reference(block_input, norm1_gain, qkv_weight, out_weight, pos_table, norm2_gain, expert_in, expert_down, lengths, routes, gate_weights, output_grad):
    buckets = jnp.asarray(bucket_table(SLOT, BUCKETS, MAX_DIST))
    weights = (norm1_gain.astype(jnp.float32), qkv_weight.astype(jnp.float32), out_weight.astype(jnp.float32), pos_table.astype(jnp.float32), norm2_gain.astype(jnp.float32), expert_in.astype(jnp.float32), expert_down.astype(jnp.float32))
    outputs = []
    input_grads = []
    totals = [jnp.zeros_like(weight) for weight in weights]
    for micro_idx in range(MICRO):
        seq_lengths = lengths[micro_idx].astype(jnp.int32)
        valid_rows = (jnp.arange(SLOT).astype(jnp.int32)[None, :] < seq_lengths[:, None]).reshape(TOKENS).astype(jnp.float32)
        route_rows = routes[micro_idx].astype(jnp.int32)
        gate_rows = gate_weights[micro_idx].astype(jnp.float32)

        def forward(residual_in, *params):
            return block_forward(residual_in, *params, seq_lengths, route_rows, gate_rows, valid_rows, buckets)
        block_out, pullback = jax.vjp(forward, block_input[micro_idx].astype(jnp.float32), *weights)
        grad_list = pullback(output_grad[micro_idx].astype(jnp.float32) * valid_rows[:, None])
        outputs.append(block_out)
        input_grads.append(grad_list[0])
        totals = [running + update for running, update in zip(totals, grad_list[1:])]
    return (jnp.stack(outputs), jnp.stack(input_grads), totals[0], totals[1], totals[2], totals[3], totals[4], totals[5], totals[6])
```

```python
import functools
import math

import jax
import jax.numpy as jnp
import numpy as np
from jax import lax
from jax.experimental import pallas as pl
from jax.experimental.pallas import tpu as pltpu
from jax.sharding import PartitionSpec as P

MAX_DIST = 128
EPSILON = 1e-06
NEG_LARGE = -1e30
BF16 = jnp.bfloat16
F32 = jnp.float32
HALF = 64
LANES = 128
GAIN_ROWS = 16
VMEM_LIMIT = 60 * 1024 * 1024


def bucket_starts(bucket_count, distance_cap):
    distance = np.arange(distance_cap + 1)
    exact_count = bucket_count // 2
    log_ratio = np.log(np.maximum(distance, 1) / exact_count) / np.log(distance_cap / exact_count)
    spread = exact_count + np.floor(
        np.maximum(log_ratio, 0.0) * (bucket_count - exact_count)
    ).astype(np.int32)
    spread = np.minimum(spread, bucket_count - 1)
    ids = np.where(distance < exact_count, distance, spread)
    return [
        int(np.argmax(ids >= b)) if (ids >= b).any() else distance_cap
        for b in range(bucket_count)
    ]


def dot(a, b):
    return lax.dot_general(a, b, (((1,), (0,)), ((), ())), preferred_element_type=F32)


def dot_nt(a, b):
    return lax.dot_general(a, b, (((1,), (1,)), ((), ())), preferred_element_type=F32)


def dot_tn(a, b):
    return lax.dot_general(a, b, (((0,), (0,)), ((), ())), preferred_element_type=F32)


def low_lanes(shape):
    return lax.broadcasted_iota(jnp.int32, shape, len(shape) - 1) < HALF


def swap_half(v):
    return pltpu.roll(v, HALF, 1)


def mix_tails(even, odd):
    lo = low_lanes(even.shape)
    return jnp.where(lo, even, swap_half(odd)), jnp.where(lo, swap_half(even), odd)


def spread_blocks(mains, tails):
    tiles = list(mains)
    for k in range(0, len(tails), 2):
        top, bottom = mix_tails(tails[k], tails[k + 1])
        tiles.append(jnp.concatenate([top, bottom], axis=0))
    return jnp.concatenate(tiles, axis=1)


def pack_blocks(wide, count):
    rows = wide.shape[0]
    mains = [wide[:, LANES * i : LANES * (i + 1)] for i in range(count)]
    tails = []
    for k in range(count // 2):
        tile = wide[:, LANES * (count + k) : LANES * (count + k + 1)]
        tails.extend(mix_tails(tile[: rows // 2], tile[rows // 2 :]))
    return mains, tails


def pack_own(own):
    rows = own.shape[0]
    tail = own[:, LANES:]
    return own[:, :LANES], jnp.concatenate([tail[: rows // 2], tail[rows // 2 :]], axis=1)


def unpack_own(main, tail):
    return jnp.concatenate(
        [main, jnp.concatenate([tail[:, :HALF], tail[:, HALF:]], axis=0)], axis=1
    )


def perm_rows(w, parts, axis):
    width = w.shape[axis] // parts
    pieces = [lax.slice_in_dim(w, width * i, width * i + LANES, axis=axis) for i in range(parts)]
    pieces += [
        lax.slice_in_dim(w, width * i + LANES, width * (i + 1), axis=axis) for i in range(parts)
    ]
    return jnp.concatenate(pieces, axis=axis)


def unperm(w, parts, axis):
    tail = w.shape[axis] // parts - LANES
    pieces = []
    for i in range(parts):
        pieces.append(lax.slice_in_dim(w, LANES * i, LANES * (i + 1), axis=axis))
        start = LANES * parts + tail * i
        pieces.append(lax.slice_in_dim(w, start, start + tail, axis=axis))
    return jnp.concatenate(pieces, axis=axis)


VM = pl.BlockSpec(memory_space=pltpu.VMEM)
SM = pl.BlockSpec(memory_space=pltpu.SMEM)
ANY = pl.BlockSpec(memory_space=pl.ANY)


def call(kernel, out_shape, in_specs, out_specs, scratch=(), flops=0, nbytes=0, name=None, **kw):
    return pl.pallas_call(
        kernel,
        out_shape=out_shape,
        in_specs=in_specs,
        out_specs=out_specs,
        scratch_shapes=list(scratch),
        compiler_params=pltpu.CompilerParams(vmem_limit_bytes=VMEM_LIMIT),
        cost_estimate=pl.CostEstimate(
            flops=int(flops), bytes_accessed=int(nbytes), transcendentals=0
        ),
        name=name,
        **kw,
    )


def sds(shape, dtype):
    return jax.ShapeDtypeStruct(tuple(shape), dtype)


def pack_kernel(x_ref, gain1_ref, gain2_ref, *rest):
    outs, rows_ref = rest[:-1], rest[-1]
    rows_ref[...] = jnp.zeros_like(rows_ref)
    for a, gain_ref in enumerate((gain1_ref, gain2_ref)):
        left = gain_ref[...]
        for p in range(3):
            part = left.astype(BF16).astype(F32)
            left = left - part
            row = 8 * a + 2 * p
            rows_ref[row : row + 1, :] = part[:, :LANES]
            rows_ref[row + 1 : row + 2, :HALF] = part[:, LANES:]
    for m, out in enumerate(outs):
        main, tail = pack_own(x_ref[m].astype(F32))
        rows = main.shape[0]
        out[:rows, :] = main.astype(BF16)
        out[rows : rows + rows // 2, :] = tail.astype(BF16)
        out[rows + rows // 2 :, :] = rows_ref[...].astype(BF16)


def pack_input(x, gain1, gain2):
    micro, slot, _ = x.shape
    total = slot + slot // 2 + GAIN_ROWS
    return call(
        pack_kernel,
        [sds((total, LANES), BF16)] * micro,
        [VM] * 3,
        [VM] * micro,
        [pltpu.VMEM((GAIN_ROWS, LANES), F32)],
        nbytes=micro * slot * 900,
        name="pack_input",
    )(x, gain1[None], gain2[None])


def wide_pair(own):
    rows = own.shape[0]
    tail = jnp.concatenate([own[:, LANES:], jnp.zeros((rows, HALF), F32)], axis=1)
    main = own[:, :LANES]
    low = jnp.concatenate([main, tail], axis=1).astype(BF16)
    high = jnp.concatenate([main, swap_half(tail)], axis=1).astype(BF16)
    return low, high


def chosen(dest_rows, first, count):
    slots = (lax.broadcasted_iota(jnp.int32, (count, dest_rows[0].shape[1]), 0) + first).astype(F32)
    hit = slots == dest_rows[0]
    for dest in dest_rows[1:]:
        hit = hit | (slots == dest)
    return jnp.where(hit, 1.0, 0.0).astype(BF16)


def dispatch_chunk(store, low, high, dests_of, first, cap):
    half = cap // 2
    top = dot(dests_of(first, half), low)
    bottom = dot(dests_of(first + half, half), high)
    store(top[:, :LANES], bottom[:, :LANES], top[:, LANES:] + bottom[:, LANES:])


def prep_kernel(
    cap, experts, len_ref, row_ref, col_ref, gate_ref, grad_ref, dy_ref, rowinfo_ref, colinfo_ref
):
    micro, slot, top_count = col_ref.shape
    half = cap // 2
    chunk = cap + half
    before = (
        lax.broadcasted_iota(jnp.int32, (slot, slot), 0)
        < lax.broadcasted_iota(jnp.int32, (slot, slot), 1)
    )
    upper = jnp.where(before, 1.0, 0.0).astype(BF16)
    after = (
        lax.broadcasted_iota(jnp.int32, (slot, slot), 1)
        < lax.broadcasted_iota(jnp.int32, (slot, slot), 0)
    )
    lower = jnp.where(after, 1.0, 0.0).astype(BF16)
    for m in range(micro):
        ids = lax.broadcasted_iota(jnp.int32, (experts, slot), 0)
        picks = [ids == row_ref[m, c : c + 1, :] for c in range(top_count)]
        named = jnp.where(picks[0] | picks[1], 1.0, 0.0).astype(BF16)
        places = dot(named, upper)
        dest_rows = []
        for c in range(top_count):
            place = jnp.sum(jnp.where(picks[c], places, 0.0), axis=0, keepdims=True)
            dest_rows.append(place + (row_ref[m, c : c + 1, :] * cap).astype(F32))
            rowinfo_ref[m, c : c + 1, :] = dest_rows[c]
        ids = lax.broadcasted_iota(jnp.int32, (slot, LANES), 1)
        picks = [ids == col_ref[m, :, c : c + 1] for c in range(top_count)]
        named = jnp.where(picks[0] | picks[1], 1.0, 0.0).astype(BF16)
        places = dot(lower, named)
        valid = jnp.where(
            lax.broadcasted_iota(jnp.int32, (slot, 1), 0) < len_ref[m, 0], 1.0, 0.0
        )
        info = jnp.where(ids == 8, valid, 0.0)
        grad = grad_ref[m].astype(F32) * valid
        lows, highs = [], []
        for c in range(top_count):
            place = jnp.sum(jnp.where(picks[c], places, 0.0), axis=1, keepdims=True)
            owner = col_ref[m, :, c : c + 1].astype(F32)
            in_low = place < half
            info = jnp.where(ids == c, owner * cap + place, info)
            info = jnp.where(ids == 2 + c, jnp.where(in_low, owner * half + place, -1.0), info)
            info = jnp.where(
                ids == 4 + c, jnp.where(in_low, -1.0, owner * half + place - half), info
            )
            gate = gate_ref[m, :, c : c + 1] * valid
            info = jnp.where(ids == 6 + c, gate, info)
            low, high = wide_pair((gate * grad).astype(BF16).astype(F32))
            lows.append(low)
            highs.append(high)
        colinfo_ref[m] = info
        low, high = jnp.concatenate(lows, axis=0), jnp.concatenate(highs, axis=0)
        base = chunk * m

        def dests_of(first, count):
            return jnp.concatenate([chosen([d], first, count) for d in dest_rows], axis=1)

        @pl.loop(0, experts)
        def _(e):
            def store(top, bottom, tail):
                dy_ref[e, base : base + half, :] = top.astype(BF16)
                dy_ref[e, base + half : base + cap, :] = bottom.astype(BF16)
                dy_ref[e, base + cap : base + chunk, :] = tail.astype(BF16)

            dispatch_chunk(store, low, high, dests_of, e * cap, cap)


def prepare(lengths, routes, gates, grads, cap, experts):
    micro, slot, top_count = routes.shape
    return call(
        functools.partial(prep_kernel, cap, experts),
        [
            sds((experts, micro * (cap + cap // 2), LANES), BF16),
            sds((micro, 8, slot), F32),
            sds((micro, slot, LANES), F32),
        ],
        [SM, VM, VM, VM, VM],
        [VM] * 3,
        flops=4e9,
        nbytes=3e6,
        name="prepare",
    )(lengths, jnp.swapaxes(routes, 1, 2), routes, gates, grads)


def stage_shards(shards, scratch, sems, me, rows=None):
    copies = []
    for j, shard in enumerate(shards):
        copies.append(pltpu.make_async_copy(shard, scratch.at[me ^ j], sems.at[j]))
    for c in copies:
        c.start()
    return copies


def load_wide(scratch, slot, parts):
    mains = [scratch[i, :slot, :].astype(F32) for i in range(parts)]
    tails = [scratch[i, slot : slot + slot // 2, :].astype(F32) for i in range(parts)]
    return spread_blocks(mains, tails)


def load_gain(scratch, first, which, parts):
    mains, tails = [], []
    for i in range(parts):
        rows = scratch[i, first : first + GAIN_ROWS, :].astype(F32)
        r = 8 * which
        mains.append(rows[r : r + 1] + rows[r + 2 : r + 3] + rows[r + 4 : r + 5])
        tails.append(rows[r + 1 : r + 2] + rows[r + 3 : r + 4] + rows[r + 5 : r + 6])
    tiles = list(mains)
    for k in range(0, parts, 2):
        tiles.append(jnp.where(low_lanes((1, LANES)), tails[k], swap_half(tails[k + 1])))
    return jnp.concatenate(tiles, axis=1)


def put_blocks(wide, scratch, keep_ref, send_ref, me, parts):
    rows = wide.shape[0]
    mains, tails = pack_blocks(wide, parts)
    for i in range(parts):
        scratch[i, :rows, :] = mains[i]
        scratch[i, rows:, :] = tails[i]
    keep_ref[0] = scratch[me]
    keep_ref[1] = scratch[me ^ 2]
    send_ref[0] = scratch[me ^ 1].astype(BF16)
    send_ref[1] = scratch[me ^ 3].astype(BF16)


def distance_tiles(block, flip):
    a = lax.broadcasted_iota(jnp.int32, (block, block), 0)
    b = lax.broadcasted_iota(jnp.int32, (block, block), 1)
    near = b - a if flip else a - b
    return near, near + block


def bias_tiles(table_ref, starts, head, block, flip):
    out = []
    for dist in distance_tiles(block, flip):
        tile = jnp.full((block, block), table_ref[0, head], F32)
        for b in range(1, len(starts)):
            tile = jnp.where(dist >= starts[b], table_ref[b, head], tile)
        out.append(tile)
    return out


def head_mask(head, width):
    lanes = lax.broadcasted_iota(jnp.int32, (1, width), 1)
    offset = (HALF * head) % LANES
    return (lanes >= offset) & (lanes < offset + HALF)


def tile_of(head):
    return (HALF * head) // LANES


def tile_slice(width, tile):
    return slice(LANES * tile, min(width, LANES * (tile + 1)))


def forward_kernel(
    starts,
    parts,
    micro_idx,
    me_ref,
    len_ref,
    table_ref,
    s0,
    s1,
    s2,
    s3,
    wq_ref,
    wo_ref,
    qkv_ref,
    att_ref,
    keep_ref,
    send_ref,
    gain_ref,
    shards,
    blocks,
    sems,
):
    me = me_ref[0]
    for c in stage_shards((s0, s1, s2, s3), shards, sems, me):
        c.wait()
    slot, pw = att_ref.shape
    heads = table_ref.shape[1]
    width = parts * pw
    block = min(LANES, slot)
    x = load_wide(shards, slot, parts)
    gain1 = load_gain(shards, slot + slot // 2, 0, parts)
    gain_ref[0:1, :] = gain1
    gain_ref[1:2, :] = load_gain(shards, slot + slot // 2, 1, parts)
    r1 = lax.rsqrt(jnp.sum(x * x, axis=1, keepdims=True) / width + EPSILON)
    n1 = (x * r1 * gain1).astype(BF16)
    for c in range(3):
        qkv_ref[c] = dot(n1, wq_ref[c]).astype(BF16)
    seq_len = len_ref[micro_idx, 0]
    scale = 1.0 / math.sqrt(pw // heads)
    tiles = sorted({tile_of(h) for h in range(heads)})
    biases = [bias_tiles(table_ref, starts, h, block, False) for h in range(heads)]
    near = distance_tiles(block, False)[0]
    for i in range(slot // block):
        keys = block * (i + 1)
        rows = slice(block * i, block * (i + 1))
        accs = {}
        key_ids = lax.broadcasted_iota(jnp.int32, (block, keys), 1)
        inside = key_ids < seq_len
        for h in range(heads):
            sl = tile_slice(pw, tile_of(h))
            tw = sl.stop - sl.start
            mask = head_mask(h, tw)
            q = jnp.where(mask, qkv_ref[0, rows, sl], 0).astype(BF16)
            s = dot_nt(q, qkv_ref[1, :keys, sl]) * scale
            parts_list = []
            for j in range(i + 1):
                sub = s[:, block * j : block * (j + 1)]
                if j == i:
                    sub = jnp.where(near >= 0, sub + biases[h][0], NEG_LARGE)
                elif j == i - 1:
                    sub = sub + biases[h][1]
                else:
                    sub = sub + table_ref[len(starts) - 1, h]
                parts_list.append(sub)
            s = jnp.concatenate(parts_list, axis=1) if i else parts_list[0]
            s = jnp.where(inside, s, NEG_LARGE)
            e = jnp.exp(s - jnp.max(s, axis=1, keepdims=True))
            p = (e / jnp.sum(e, axis=1, keepdims=True)).astype(BF16)
            v = jnp.where(mask, qkv_ref[2, :keys, sl], 0).astype(BF16)
            got = dot(p, v)
            accs[tile_of(h)] = accs[tile_of(h)] + got if tile_of(h) in accs else got
        for tile in tiles:
            att_ref[rows, tile_slice(pw, tile)] = accs[tile].astype(BF16)
    put_blocks(dot(att_ref[...], wo_ref[...]), blocks, keep_ref, send_ref, me, parts)


def forward(me, lengths, table, shards, wq, wo, micro_idx, starts):
    parts = len(shards)
    packed = shards[0].shape[0]
    slot = (packed - GAIN_ROWS) * 2 // 3
    pw = wq.shape[2]
    rows = slot + slot // 2
    return call(
        functools.partial(forward_kernel, starts, parts, micro_idx),
        [
            sds((3, slot, pw), BF16),
            sds((slot, pw), BF16),
            sds((2, rows, LANES), F32),
            sds((2, rows, LANES), BF16),
            sds((2, parts * pw), F32),
        ],
        [SM, SM, SM] + [ANY] * parts + [VM, VM],
        [VM] * 5,
        [
            pltpu.VMEM((parts, packed, LANES), BF16),
            pltpu.VMEM((parts, rows, LANES), F32),
            pltpu.SemaphoreType.DMA((parts,)),
        ],
        flops=4e9,
        nbytes=6e6,
        name=f"forward_{micro_idx}",
    )(me, lengths, table, *shards, wq, wo)


def middle_kernel(
    cap, experts, x_ref, keep_ref, got_core_ref, got_x_ref, info_ref, mid_ref, send_ref
):
    rows = mid_ref.shape[0]
    slot = rows * 2 // 3
    half = cap // 2
    mid = (
        x_ref[:rows, :].astype(F32)
        + keep_ref[0]
        + got_core_ref[0].astype(F32)
        + got_x_ref[...].astype(F32)
    )
    mid_ref[...] = mid
    main, tail = mid[:slot], mid[slot:]
    lo = low_lanes(tail.shape)
    tail_low = jnp.concatenate(
        [jnp.where(lo, tail, 0.0), jnp.where(lo, swap_half(tail), 0.0)], axis=0
    )
    tail_high = jnp.concatenate(
        [jnp.where(lo, 0.0, swap_half(tail)), jnp.where(lo, 0.0, tail)], axis=0
    )
    low = jnp.concatenate([main, tail_low], axis=1).astype(BF16)
    high = jnp.concatenate([main, tail_high], axis=1).astype(BF16)
    dest_rows = [info_ref[0, c : c + 1, :] for c in range(2)]

    @pl.loop(0, experts)
    def _(e):
        def store(top, bottom, tail):
            send_ref[e, :half, :] = top.astype(BF16)
            send_ref[e, half:cap, :] = bottom.astype(BF16)
            send_ref[e, cap:, :] = tail.astype(BF16)

        dispatch_chunk(
            store, low, high, lambda first, count: chosen(dest_rows, first, count), e * cap, cap
        )


def middle(x_packed, keep, got_core, got_x, rowinfo, micro_idx, cap, experts):
    rows = keep.shape[1]
    slot = rows * 2 // 3
    first = pl.BlockSpec((1, rows, LANES), lambda i: (0, 0, 0))
    whole2 = lambda a: pl.BlockSpec(a.shape, lambda i: (0, 0))
    return call(
        functools.partial(middle_kernel, cap, experts),
        [sds((rows, LANES), F32), sds((experts, cap + cap // 2, LANES), BF16)],
        [
            whole2(x_packed),
            first,
            first,
            whole2(got_x),
            pl.BlockSpec((1, 8, slot), lambda i: (micro_idx, 0, 0)),
        ],
        [
            pl.BlockSpec((rows, LANES), lambda i: (0, 0)),
            pl.BlockSpec((experts, cap + cap // 2, LANES), lambda i: (0, 0, 0)),
        ],
        grid=(1,),
        flops=1e9,
        nbytes=2e6,
        name=f"middle_{micro_idx}",
    )(x_packed, keep, got_core, got_x, rowinfo)


def load_rows(scratch, step, spread, cap, parts):
    mains, tails = [], []
    half = cap // 2
    for i in range(parts):
        ref = scratch.at[i, pl.ds(step * spread, spread)]
        mains.append(ref[:, :cap, :].astype(F32).reshape(spread * cap, LANES))
        tails.append(ref[:, cap:, :].astype(F32).reshape(spread * half, LANES))
    tiles = list(mains)
    for k in range(0, parts, 2):
        top, bottom = mix_tails(tails[k], tails[k + 1])
        tiles.append(
            jnp.concatenate(
                [top.reshape(spread, half, LANES), bottom.reshape(spread, half, LANES)], axis=1
            ).reshape(spread * cap, LANES)
        )
    return jnp.concatenate(tiles, axis=1)


def put_rows(wide, scratch, keep_ref, send_ref, me, spread, cap, parts):
    half = cap // 2
    for i in range(parts):
        scratch[i, :, :cap, :] = wide[:, LANES * i : LANES * (i + 1)].reshape(spread, cap, LANES)
    for k in range(parts // 2):
        tile = wide[:, LANES * (parts + k) : LANES * (parts + k + 1)].reshape(spread, cap, LANES)
        top = tile[:, :half].reshape(spread * half, LANES)
        bottom = tile[:, half:].reshape(spread * half, LANES)
        even, odd = mix_tails(top, bottom)
        scratch[2 * k, :, cap:, :] = even.reshape(spread, half, LANES)
        scratch[2 * k + 1, :, cap:, :] = odd.reshape(spread, half, LANES)
    keep_ref[0] = scratch[me]
    keep_ref[1] = scratch[me ^ 2]
    send_ref[0] = scratch[me ^ 1].astype(BF16)
    send_ref[1] = scratch[me ^ 3].astype(BF16)


def expert_kernel(
    parts,
    spread,
    cap,
    dy_base,
    me_ref,
    m0,
    m1,
    m2,
    m3,
    d0,
    d1,
    d2,
    d3,
    win_ref,
    wdown_ref,
    gain_ref,
    n2_ref,
    act_ref,
    dpre_ref,
    dy_ref,
    keep_ref,
    send_ref,
    gsum_ref,
    mid_s,
    dy_s,
    blocks,
    sems,
):
    me = me_ref[0]
    step = pl.program_id(0)
    steps = pl.num_programs(0)
    chunk = cap + cap // 2

    def copies(at):
        out = []
        for j, (mid, dy) in enumerate(((m0, d0), (m1, d1), (m2, d2), (m3, d3))):
            part = pl.ds(at * spread, spread)
            out.append(
                pltpu.make_async_copy(mid.at[part], mid_s.at[me ^ j, part], sems.at[0, j, at])
            )
            out.append(
                pltpu.make_async_copy(
                    dy.at[part, pl.ds(dy_base, chunk)], dy_s.at[me ^ j, part], sems.at[1, j, at]
                )
            )
        return out

    @pl.when(step == 0)
    def _():
        @pl.loop(0, steps)
        def _(at):
            for c in copies(at):
                c.start()

        gsum_ref[...] = jnp.zeros_like(gsum_ref)

    for c in copies(step):
        c.wait()
    width = win_ref.shape[0]
    mid = load_rows(mid_s, step, spread, cap, parts)
    dy = load_rows(dy_s, step, spread, cap, parts).astype(BF16)
    gain = gain_ref[1:2, :]
    r2 = lax.rsqrt(jnp.sum(mid * mid, axis=1, keepdims=True) / width + EPSILON)
    xr = mid * r2
    n2 = (xr * gain).astype(BF16)
    pre = dot(n2, win_ref[...])
    erf = lax.erf(pre * (1.0 / math.sqrt(2.0)))
    cdf = 0.5 * (1.0 + erf)
    act_ref[...] = (pre * cdf).astype(BF16)
    slope = cdf + pre * (jnp.exp(-0.5 * pre * pre) * (1.0 / math.sqrt(2.0 * math.pi)))
    dact = dot_nt(dy, wdown_ref[...])
    dpre = (dact * slope).astype(BF16)
    inner = jnp.sum(dpre.astype(F32) * pre, axis=1, keepdims=True)
    dn2 = dot_nt(dpre, win_ref[...])
    n2_ref[...] = n2
    dy_ref[...] = dy
    dpre_ref[...] = dpre
    gsum_ref[0:1, :] += jnp.sum(dn2 * xr, axis=0, keepdims=True)
    drow = r2 * (dn2 * gain) - xr * (r2 * inner * (1.0 / width))
    put_rows(drow, blocks, keep_ref, send_ref, me, spread, cap, parts)


def row_spread(owners, cap):
    best = 1
    for s in range(1, owners + 1):
        if owners % s == 0 and s * cap <= 320:
            best = s
    return best


def expert_main(me, mids, dys, win, wdown, gains, micro_idx, cap):
    parts = len(mids)
    owners, chunk, _ = mids[0].shape
    width, hidden = win.shape
    spread = row_spread(owners, cap)
    steps = owners // spread
    total = owners * cap
    rows = spread * cap
    by_row = lambda w: pl.BlockSpec((rows, w), lambda i: (i, 0))
    full = lambda a: pl.BlockSpec(a.shape, lambda i: (0,) * a.ndim)
    blocks = pl.BlockSpec((2, spread, chunk, LANES), lambda i: (0, i, 0, 0))
    return call(
        functools.partial(expert_kernel, parts, spread, cap, chunk * micro_idx),
        [
            sds((total, width), BF16),
            sds((total, hidden), BF16),
            sds((total, hidden), BF16),
            sds((total, width), BF16),
            sds((2, owners, chunk, LANES), F32),
            sds((2, owners, chunk, LANES), BF16),
            sds((8, width), F32),
        ],
        [SM] + [ANY] * (2 * parts) + [full(win), full(wdown), full(gains)],
        [
            by_row(width),
            by_row(hidden),
            by_row(hidden),
            by_row(width),
            blocks,
            blocks,
            pl.BlockSpec((8, width), lambda i: (0, 0)),
        ],
        [
            pltpu.VMEM((parts, owners, chunk, LANES), BF16),
            pltpu.VMEM((parts, owners, chunk, LANES), BF16),
            pltpu.VMEM((parts, spread, chunk, LANES), F32),
            pltpu.SemaphoreType.DMA((2, parts, steps)),
        ],
        grid=(steps,),
        flops=6 * total * width * hidden,
        nbytes=2e7,
        name=f"expert_{micro_idx}",
    )(me, *mids, *dys, win, wdown, gains)


def down_kernel(parts, spread, cap, me_ref, act_ref, wdown_ref, keep_ref, send_ref, blocks):
    put_rows(
        dot(act_ref[...], wdown_ref[...]), blocks, keep_ref, send_ref, me_ref[0], spread, cap, parts
    )


def expert_down_rows(me, act, wdown, owners, parts, micro_idx, cap):
    total, hidden = act.shape
    width = wdown.shape[1]
    chunk = cap + cap // 2
    spread = row_spread(owners, cap)
    rows = spread * cap
    blocks = pl.BlockSpec((2, spread, chunk, LANES), lambda i: (0, i, 0, 0))
    return call(
        functools.partial(down_kernel, parts, spread, cap),
        [
            sds((2, owners, chunk, LANES), F32),
            sds((2, owners, chunk, LANES), BF16),
        ],
        [
            SM,
            pl.BlockSpec((rows, hidden), lambda i: (i, 0)),
            pl.BlockSpec(wdown.shape, lambda i: (0, 0)),
        ],
        [blocks, blocks],
        [pltpu.VMEM((parts, spread, chunk, LANES), F32)],
        grid=(owners // spread,),
        flops=2 * total * width * hidden,
        nbytes=1e7,
        name=f"down_{micro_idx}",
    )(me, act, wdown)


def picked_rows(rows_ref, info, cap, pairs, weights=None):
    owners = rows_ref.shape[0]
    slot = info.shape[0]
    half = cap // 2
    mains = rows_ref[:, :cap, :].reshape(owners * cap, LANES)
    tails = rows_ref[:, cap:, :].reshape(owners * half, LANES)

    def hits(columns, count):
        ids = lax.broadcasted_iota(jnp.int32, (slot, count), 1).astype(F32)
        hit = ids == info[:, columns[0] : columns[0] + 1]
        for c in columns[1:]:
            hit = hit | (ids == info[:, c : c + 1])
        return jnp.where(hit, 1.0, 0.0).astype(BF16)

    main = dot(hits(pairs, owners * cap), mains)
    low = dot(hits([2 + c for c in pairs], owners * half), tails)
    high = dot(hits([4 + c for c in pairs], owners * half), tails)
    lo = low_lanes(low.shape)
    tail = jnp.where(lo, low + swap_half(high), 0.0)
    return main, tail


def pack_tail(tail):
    rows = tail.shape[0]
    return tail[: rows // 2] + swap_half(tail[rows // 2 :])


def dmid_kernel(cap, rows_ref, info_ref, grad_ref, dmid_ref, low_ref):
    info = info_ref[0]
    slot = info.shape[0]
    main, tail = picked_rows(rows_ref, info, cap, [0, 1])
    grad = grad_ref[0].astype(F32) * info[:, 8:9]
    gmain, gtail = pack_own(grad)
    main = main + gmain
    tail = pack_tail(tail) + gtail
    dmid_ref[:slot, :] = main
    dmid_ref[slot:, :] = tail
    low_ref[:slot, :] = main.astype(BF16)
    low_ref[slot:, :] = tail.astype(BF16)


def mid_gradient(rows, colinfo, grads, micro_idx, cap):
    micro, slot, pw = grads.shape
    packed = slot + slot // 2
    return call(
        functools.partial(dmid_kernel, cap),
        [sds((packed, LANES), F32), sds((packed, LANES), BF16)],
        [
            pl.BlockSpec(rows.shape, lambda i: (0, 0, 0)),
            pl.BlockSpec((1, slot, LANES), lambda i: (micro_idx, 0, 0)),
            pl.BlockSpec((1, slot, pw), lambda i: (micro_idx, 0, 0)),
        ],
        [pl.BlockSpec((packed, LANES), lambda i: (0, 0))] * 2,
        grid=(1,),
        flops=1e9,
        nbytes=2e6,
        name=f"dmid_{micro_idx}",
    )(rows, colinfo, grads)


def output_kernel(cap, rows_ref, info_ref, mid_ref, out_ref):
    info = info_ref[0]
    slot = info.shape[0]
    main, tail = mid_ref[:slot, :], None
    for c in range(2):
        got_main, got_tail = picked_rows(rows_ref, info, cap, [c])
        gate = info[:, 6 + c : 7 + c]
        main = main + gate * got_main
        tail = gate * got_tail if tail is None else tail + gate * got_tail
    out_ref[...] = unpack_own(main, mid_ref[slot:, :] + pack_tail(tail))


def block_result(rows, colinfo, mid, micro_idx, cap, pw):
    packed = mid.shape[0]
    slot = packed * 2 // 3
    return call(
        functools.partial(output_kernel, cap),
        sds((slot, pw), F32),
        [
            pl.BlockSpec(rows.shape, lambda i: (0, 0, 0)),
            pl.BlockSpec((1, slot, LANES), lambda i: (micro_idx, 0, 0)),
            pl.BlockSpec((packed, LANES), lambda i: (0, 0)),
        ],
        pl.BlockSpec((slot, pw), lambda i: (0, 0)),
        grid=(1,),
        flops=1e9,
        nbytes=2e6,
        name=f"output_{micro_idx}",
    )(rows, colinfo, mid)


def backward_kernel(
    starts,
    parts,
    micro_idx,
    first,
    last,
    me_ref,
    len_ref,
    table_ref,
    d0,
    d1,
    d2,
    d3,
    s0,
    s1,
    s2,
    s3,
    qkv_ref,
    att_ref,
    wq_ref,
    wo_ref,
    gain_ref,
    *rest,
):
    if first:
        prior = None
    else:
        prior, rest = rest[:4], rest[4:]
    keep_ref, send_ref, gq_ref, go_ref, diag_ref, small_ref, *rest = rest
    if last:
        pos_ref, *rest = rest
    datt_s, x_s, blocks, dqkv_s, sems, pos_s = rest
    me = me_ref[0]
    waits = stage_shards((d0, d1, d2, d3), datt_s, sems.at[0], me)
    waits += stage_shards((s0, s1, s2, s3), x_s, sems.at[1], me)
    for c in waits:
        c.wait()
    slot, pw = att_ref.shape
    heads = table_ref.shape[1]
    width = parts * pw
    block = min(LANES, slot)
    seq_len = len_ref[micro_idx, 0]
    scale = 1.0 / math.sqrt(pw // heads)

    dout = load_wide(datt_s, slot, parts).astype(BF16)
    datt = dot_nt(dout, wo_ref[...]).astype(BF16)
    go = dot_tn(att_ref[...], dout)

    dqkv_s[...] = jnp.zeros_like(dqkv_s)
    near = distance_tiles(block, True)[0]
    far_sums = []
    for h in range(heads):
        sl = tile_slice(pw, tile_of(h))
        mask = head_mask(h, sl.stop - sl.start)
        near_bias, next_bias = bias_tiles(table_ref, starts, h, block, True)
        near_sum = jnp.zeros((block, block), F32)
        next_sum = jnp.zeros((block, block), F32)
        far_sum = jnp.zeros((1, block), F32)
        k_masked = jnp.where(mask, qkv_ref[1, :, sl], 0).astype(BF16)
        for i in range(slot // block):
            keys = block * (i + 1)
            rows = slice(block * i, block * (i + 1))
            q = jnp.where(mask, qkv_ref[0, rows, sl], 0).astype(BF16)
            da = jnp.where(mask, datt[rows, sl], 0).astype(BF16)
            s = dot_nt(qkv_ref[1, :keys, sl], q) * scale
            pieces = []
            for j in range(i + 1):
                sub = s[block * j : block * (j + 1)]
                if j == i:
                    sub = jnp.where(near >= 0, sub + near_bias, NEG_LARGE)
                elif j == i - 1:
                    sub = sub + next_bias
                else:
                    sub = sub + table_ref[len(starts) - 1, h]
                pieces.append(sub)
            s = jnp.concatenate(pieces, axis=0) if i else pieces[0]
            inside = lax.broadcasted_iota(jnp.int32, (keys, block), 0) < seq_len
            s = jnp.where(inside, s, NEG_LARGE)
            e = jnp.exp(s - jnp.max(s, axis=0, keepdims=True))
            p = e / jnp.sum(e, axis=0, keepdims=True)
            dp = dot_nt(qkv_ref[2, :keys, sl], da)
            delta = jnp.sum(dp * p, axis=0, keepdims=True)
            ds = (p * (dp - delta)).astype(BF16)
            dqkv_s[2, :keys, sl] += dot(p.astype(BF16), da)
            dqkv_s[1, :keys, sl] += dot(ds, q)
            dqkv_s[0, rows, sl] += dot_tn(ds, k_masked[:keys])
            wide = ds.astype(F32)
            near_sum = near_sum + wide[block * i :]
            if i >= 1:
                next_sum = next_sum + wide[block * (i - 1) : block * i]
            if i >= 2:
                far_sum = far_sum + jnp.sum(wide[: block * (i - 1)], axis=0, keepdims=True)
        if prior is not None:
            near_sum = near_sum + prior[2][2 * h]
            next_sum = next_sum + prior[2][2 * h + 1]
            far_sum = far_sum + prior[3][8 + h : 9 + h, :block]
        if last:
            near_d, next_d = distance_tiles(block, True)
            count = len(starts)
            for b in range(count):
                row = jnp.zeros((1, block), F32)
                for dist, total in ((near_d, near_sum), (next_d, next_sum)):
                    hit = dist >= starts[b]
                    if b + 1 < count:
                        hit = hit & (dist < starts[b + 1])
                    row = row + jnp.sum(jnp.where(hit, total, 0.0), axis=0, keepdims=True)
                if b + 1 == count:
                    row = row + far_sum
                pos_s[h, b : b + 1, :] = row
        else:
            diag_ref[2 * h] = near_sum
            diag_ref[2 * h + 1] = next_sum
        far_sums.append(far_sum)

    gain1 = gain_ref[0:1, :]
    x = load_wide(x_s, slot, parts)
    r1 = lax.rsqrt(jnp.sum(x * x, axis=1, keepdims=True) / width + EPSILON)
    xr = x * r1
    n1 = (xr * gain1).astype(BF16)
    inner = jnp.zeros((slot, 1), F32)
    dn1 = jnp.zeros((slot, width), F32)
    for c in range(3):
        d = dqkv_s[c]
        if c < 2:
            d = d * scale
        low = d.astype(BF16)
        inner = inner + jnp.sum(
            low.astype(F32) * qkv_ref[c].astype(F32), axis=1, keepdims=True
        )
        dn1 = dn1 + dot_nt(low, wq_ref[c])
        gq = dot_tn(n1, low)
        if prior is not None:
            gq = gq + prior[0][c]
        if last:
            rows = gq.shape[0]
            base = c * (rows + rows // 2)
            main, tail = pack_own(gq)
            gq_ref[base : base + rows, :] = main.astype(BF16)
            gq_ref[base + rows : base + rows + rows // 2, :] = tail.astype(BF16)
        else:
            gq_ref[c] = gq
    if prior is not None:
        go = go + prior[1][...]
    if last:
        for k in range(width // LANES):
            go_ref[pw * k : pw * (k + 1), :] = go[:, LANES * k : LANES * (k + 1)].astype(BF16)
    else:
        go_ref[...] = go
    small_ref[...] = jnp.zeros_like(small_ref)
    gain_sum = jnp.sum(dn1 * xr, axis=0, keepdims=True)
    if prior is not None:
        gain_sum = gain_sum + prior[3][0:1, :]
    small_ref[0:1, :] = gain_sum
    if last:
        for h in range(heads):
            pos_ref[:, h : h + 1] = jnp.sum(pos_s[h], axis=1, keepdims=True)
        pos_ref[:, heads:] = jnp.zeros((pos_ref.shape[0], LANES - heads), F32)
    else:
        for h in range(heads):
            small_ref[8 + h : 9 + h, :block] = far_sums[h]
    out = r1 * (dn1 * gain1) - xr * (r1 * inner * (1.0 / width))
    put_blocks(out, blocks, keep_ref, send_ref, me, parts)


def backward(me, lengths, table, dshards, xshards, qkv, att, wq, wo, gains, prior, micro_idx, last, starts):
    parts = len(dshards)
    slot, pw = att.shape
    width = parts * pw
    packed = slot + slot // 2
    block = min(LANES, slot)
    heads = table.shape[1]
    buckets = table.shape[0]
    outs = [sds((2, packed, LANES), F32), sds((2, packed, LANES), BF16)]
    if last:
        outs += [
            sds((3 * (width + width // 2), LANES), BF16),
            sds((width // LANES * pw, LANES), BF16),
        ]
    else:
        outs += [sds((3, width, pw), F32), sds((pw, width), F32)]
    outs += [sds((2 * heads, block, block), F32), sds((16, width), F32)]
    if last:
        outs.append(sds((buckets, LANES), F32))
    first = prior is None
    extra = () if first else tuple(prior)
    return call(
        functools.partial(backward_kernel, starts, parts, micro_idx, first, last),
        outs,
        [SM, SM, SM] + [ANY] * (2 * parts) + [VM] * (5 + len(extra)),
        [VM] * len(outs),
        [
            pltpu.VMEM((parts,) + dshards[0].shape, BF16),
            pltpu.VMEM((parts,) + xshards[0].shape, BF16),
            pltpu.VMEM((parts, packed, LANES), F32),
            pltpu.VMEM((3, slot, pw), F32),
            pltpu.SemaphoreType.DMA((2, parts)),
            pltpu.VMEM((heads, buckets, block), F32),
        ],
        flops=8e9,
        nbytes=1e7,
        name=f"backward_{micro_idx}",
    )(me, lengths, table, *dshards, *xshards, qkv, att, wq, wo, gains, *extra)


def final_kernel(dmid_ref, keep_ref, got_core_ref, got_x_ref, out_ref):
    slot = out_ref.shape[0]
    total = (
        dmid_ref[...] + keep_ref[0] + got_core_ref[0].astype(F32) + got_x_ref[...].astype(F32)
    )
    out_ref[...] = unpack_own(total[:slot], total[slot:])


def input_gradient(dmid, keep, got_core, got_x, micro_idx, pw):
    packed = dmid.shape[0]
    slot = packed * 2 // 3
    first = pl.BlockSpec((1, packed, LANES), lambda i: (0, 0, 0))
    whole = pl.BlockSpec((packed, LANES), lambda i: (0, 0))
    return call(
        final_kernel,
        sds((slot, pw), F32),
        [whole, first, first, whole],
        pl.BlockSpec((slot, pw), lambda i: (0, 0)),
        grid=(1,),
        nbytes=2e6,
        name=f"final_{micro_idx}",
    )(dmid, keep, got_core, got_x)


def swap(value, flip):
    count = lax.axis_size("tensor")
    return lax.ppermute(value, "tensor", [(i, i ^ flip) for i in range(count)])


def gather_shards(own):
    across = swap(own, 2)
    beside = swap(own, 1)
    far = swap(across, 1)
    return (own, beside, across, far)


def exchange(value):
    return lax.all_to_all(value, "expert", split_axis=0, concat_axis=0, tiled=True)


def reduce_blocks(keep, send):
    got_core = swap(send, 1)
    onward = (keep[1] + got_core[1].astype(F32)).astype(BF16)
    return got_core, swap(onward, 2)


def reduce_rows(keep, send):
    got_core, got_x = reduce_blocks(keep, send)
    return (keep[0] + got_core[0].astype(F32) + got_x.astype(F32)).astype(BF16)


def pad_rows(value, multiple):
    short = -value.shape[0] % multiple
    return jnp.pad(value, ((0, short), (0, 0))) if short else value


def sum_over_experts(value):
    owners = lax.axis_size("expert")
    value = pad_rows(value, 16 * owners)
    got = exchange(value.reshape(owners, -1, LANES))
    return jnp.sum(got.astype(F32), axis=0)


def spread_over_experts(block):
    owners = lax.axis_size("expert")
    return exchange(jnp.broadcast_to(block[None], (owners,) + block.shape))


def local(
    block_input,
    norm1_gain,
    qkv_weight,
    out_weight,
    pos_table,
    norm2_gain,
    expert_in,
    expert_down,
    lengths,
    routes,
    gate_weights,
    output_grad,
):
    micro_count, slot_len, pw = block_input.shape
    parts = lax.axis_size("tensor")
    owners = lax.axis_size("expert")
    experts = expert_in.shape[0] * owners
    assert parts == 4 and expert_in.shape[0] == 1 and pw == LANES + HALF
    width = parts * pw
    top_count = routes.shape[2]
    need = max(2, 5 * slot_len * top_count // (4 * experts))
    cap = -(-need // 32) * 32
    bucket_count, heads = pos_table.shape
    starts = bucket_starts(bucket_count, MAX_DIST)
    me = lax.axis_index("tensor").astype(jnp.int32)[None]

    packed = pack_input(block_input, norm1_gain, norm2_gain)
    xshards = [gather_shards(p) for p in packed]
    dy_send, rowinfo, colinfo = prepare(
        lengths, routes, gate_weights, output_grad, cap, experts
    )
    dys = gather_shards(exchange(dy_send))

    wq = perm_rows(qkv_weight, parts, 1)
    wo = perm_rows(out_weight, parts, 1)
    win = perm_rows(expert_in[0], parts, 0)
    wdown = perm_rows(expert_down[0], parts, 1)

    fwd, mids, rows_in = [], [], []
    for m in range(micro_count):
        qkv, att, keep, send, gains = forward(
            me, lengths, pos_table, xshards[m], wq, wo, m, starts
        )
        got_core, got_x = reduce_blocks(keep, send)
        mid, to_experts = middle(
            packed[m], keep, got_core, got_x, rowinfo, m, cap, experts
        )
        fwd.append((qkv, att, gains))
        mids.append(mid)
        rows_in.append(gather_shards(exchange(to_experts)))

    expert_out, dmids = [], []
    for m in range(micro_count):
        n2, act, dpre, dy, keep, send, gsum = expert_main(
            me, rows_in[m], dys, win, wdown, fwd[m][2], m, cap
        )
        expert_out.append((n2, act, dpre, dy, gsum))
        back = exchange(reduce_rows(keep, send))
        dmids.append(mid_gradient(back, colinfo, output_grad, m, cap))

    outputs = []
    for m in range(micro_count):
        keep, send = expert_down_rows(me, expert_out[m][1], wdown, owners, parts, m, cap)
        back = exchange(reduce_rows(keep, send))
        outputs.append(block_result(back, colinfo, mids[m], m, cap, pw))

    grad_in = sum(
        lax.dot_general(n2, dpre, (((0,), (0,)), ((), ())), preferred_element_type=F32)
        for n2, _, dpre, _, _ in expert_out
    )
    grad_down = sum(
        lax.dot_general(act, dy, (((0,), (0,)), ((), ())), preferred_element_type=F32)
        for _, act, _, dy, _ in expert_out
    )

    prior, input_grads = None, []
    for m in range(micro_count):
        dmid, low = dmids[m]
        last = m == micro_count - 1
        qkv, att, gains = fwd[m]
        keep, send, gq, go, diag, small, *pos = backward(
            me, lengths, pos_table, gather_shards(low), xshards[m], qkv, att, wq, wo, gains,
            prior, m, last, starts,
        )
        prior = (gq, go, diag, small)
        got_core, got_x = reduce_blocks(keep, send)
        input_grads.append(input_gradient(dmid, keep, got_core, got_x, m, pw))

    sums = jnp.stack([small[0], sum(e[4][0] for e in expert_out)])
    sums = unperm(sums, parts, 1)
    sums = sums + swap(sums, 2)
    sums = sums + swap(sums, 1)
    own = lax.dynamic_slice_in_dim(sums, me[0] * pw, pw, 1)
    flat = jnp.concatenate([own.reshape(-1), pos[0][:, :heads].reshape(-1)])
    flat = jnp.pad(flat, (0, -flat.shape[0] % (8 * LANES))).reshape(-1, LANES)
    high = flat.astype(BF16)
    rest = (flat - high.astype(F32)).astype(BF16)
    tiny = jnp.concatenate([high, rest], axis=0)

    gq_rows = gq.shape[0]
    go_rows = go.shape[0]
    gq_sum = sum_over_experts(gq).astype(BF16)
    go_sum = sum_over_experts(go).astype(BF16)
    sent = jnp.concatenate([gq_sum, go_sum, tiny], axis=0)
    got = spread_over_experts(sent)
    a, b = gq_sum.shape[0], go_sum.shape[0]
    gq_all = got[:, :a].reshape(-1, LANES)[:gq_rows].reshape(3, width + width // 2, LANES)
    go_all = got[:, a : a + b].reshape(-1, LANES)[:go_rows].reshape(width // LANES, pw, LANES)
    tiny_all = jnp.sum(got[:, a + b :].astype(F32), axis=0)
    flat = (tiny_all[: high.shape[0]] + tiny_all[high.shape[0] :]).reshape(-1)
    gq_tail = gq_all[:, width:]
    gq_full = jnp.concatenate(
        [
            gq_all[:, :width],
            jnp.concatenate([gq_tail[:, :, :HALF], gq_tail[:, :, HALF:]], axis=1),
        ],
        axis=2,
    )
    grad_qkv = unperm(gq_full, parts, 1).astype(F32)
    grad_out = unperm(jnp.swapaxes(go_all, 0, 1).reshape(pw, width), parts, 1).astype(F32)
    return (
        jnp.stack(outputs),
        jnp.stack(input_grads),
        flat[:pw],
        grad_qkv,
        grad_out,
        flat[2 * pw : 2 * pw + bucket_count * heads].reshape(bucket_count, heads),
        flat[pw : 2 * pw],
        unperm(grad_in, parts, 0)[None],
        unperm(grad_down, parts, 1)[None],
    )


def solution(mesh):
    in_specs = (
        P(None, "expert", "tensor"),
        P("tensor"),
        P(None, None, "tensor"),
        P("tensor", None),
        P(None, "tensor"),
        P("tensor"),
        P("expert", None, "tensor"),
        P("expert", "tensor", None),
        P(None, "expert"),
        P(None, "expert", None),
        P(None, "expert", None),
        P(None, "expert", "tensor"),
    )
    out_specs = (
        P(None, "expert", "tensor"),
        P(None, "expert", "tensor"),
        P("tensor"),
        P(None, None, "tensor"),
        P("tensor", None),
        P(None, "tensor"),
        P("tensor"),
        P("expert", None, "tensor"),
        P("expert", "tensor", None),
    )
    return jax.shard_map(local, mesh=mesh, in_specs=in_specs, out_specs=out_specs, check_vma=False)
```

```python
import functools
import math

import jax
import jax.numpy as jnp
import numpy as np
from jax import lax
from jax.experimental import pallas as pl
from jax.experimental.pallas import tpu as pltpu
from jax.sharding import PartitionSpec as P

MAX_DIST = 128
EPSILON = 1e-06
NEG_LARGE = -1e30
BF16 = jnp.bfloat16
F32 = jnp.float32
HALF = 64
LANES = 128
GAIN_WIDTH = 256
VMEM_LIMIT = 60 * 1024 * 1024


def bucket_starts(bucket_count, distance_cap):
    distance = np.arange(distance_cap + 1)
    exact_count = bucket_count // 2
    log_ratio = np.log(np.maximum(distance, 1) / exact_count) / np.log(distance_cap / exact_count)
    spread = exact_count + np.floor(
        np.maximum(log_ratio, 0.0) * (bucket_count - exact_count)
    ).astype(np.int32)
    spread = np.minimum(spread, bucket_count - 1)
    ids = np.where(distance < exact_count, distance, spread)
    return [
        int(np.argmax(ids >= b)) if (ids >= b).any() else distance_cap
        for b in range(bucket_count)
    ]


def dot(a, b):
    return lax.dot_general(a, b, (((1,), (0,)), ((), ())), preferred_element_type=F32)


def dot_nt(a, b):
    return lax.dot_general(a, b, (((1,), (1,)), ((), ())), preferred_element_type=F32)


def dot_tn(a, b):
    return lax.dot_general(a, b, (((0,), (0,)), ((), ())), preferred_element_type=F32)


def low_lanes(shape):
    return lax.broadcasted_iota(jnp.int32, shape, len(shape) - 1) < HALF


def swap_half(v):
    return pltpu.roll(v, HALF, 1)


def mix_tails(even, odd):
    lo = low_lanes(even.shape)
    return jnp.where(lo, even, swap_half(odd)), jnp.where(lo, swap_half(even), odd)


VM = pl.BlockSpec(memory_space=pltpu.VMEM)
SM = pl.BlockSpec(memory_space=pltpu.SMEM)
ANY = pl.BlockSpec(memory_space=pl.ANY)


def call(kernel, out_shape, in_specs, out_specs, scratch=(), flops=0, nbytes=0, name=None, **kw):
    return pl.pallas_call(
        kernel,
        out_shape=out_shape,
        in_specs=in_specs,
        out_specs=out_specs,
        scratch_shapes=list(scratch),
        compiler_params=pltpu.CompilerParams(vmem_limit_bytes=VMEM_LIMIT),
        cost_estimate=pl.CostEstimate(
            flops=int(flops), bytes_accessed=int(nbytes), transcendentals=0
        ),
        name=name,
        **kw,
    )


def sds(shape, dtype):
    return jax.ShapeDtypeStruct(tuple(shape), dtype)


def at(a, *index):
    rest = a.ndim - len(index)
    return pl.BlockSpec((1,) * len(index) + a.shape[len(index) :], lambda i: index + (0,) * rest)


def whole(a):
    return pl.BlockSpec(a.shape, lambda i: (0,) * len(a.shape))


def main_first(me):
    return pl.multiple_of((me & 1) * HALF, HALF)


def tail_first(me):
    return pl.multiple_of((1 - (me & 1)) * LANES, HALF)


def wide_pair(main, tail):
    zero = jnp.zeros_like(tail)
    return (
        jnp.concatenate([main, tail, zero], axis=0).astype(BF16),
        jnp.concatenate([main, zero, tail], axis=0).astype(BF16),
    )


def chosen(dest_rows, first, count):
    slots = (lax.broadcasted_iota(jnp.int32, (count, dest_rows[0].shape[1]), 0) + first).astype(F32)
    hit = slots == dest_rows[0]
    for dest in dest_rows[1:]:
        hit = hit | (slots == dest)
    return jnp.where(hit, 1.0, 0.0).astype(BF16)


def dispatch(send_ref, pairs, dests, cap):
    experts = send_ref.shape[0]
    half = cap // 2

    @pl.loop(0, experts)
    def _(e):
        top = bottom = None
        for (low, high), dest in zip(pairs, dests):
            a = dot_nt(chosen(dest, e * cap, half), low)
            b = dot_nt(chosen(dest, e * cap + half, half), high)
            top = a if top is None else top + a
            bottom = b if bottom is None else bottom + b
        send_ref[e, :half, :] = top[:, :LANES].astype(BF16)
        send_ref[e, half:cap, :] = bottom[:, :LANES].astype(BF16)
        send_ref[e, cap:, :] = (top[:, LANES:] + bottom[:, LANES:]).astype(BF16)


def routes_kernel(cap, experts, len_ref, route_ref, gate_ref, info_ref):
    micro, top_count, slot = route_ref.shape
    before = (
        lax.broadcasted_iota(jnp.int32, (slot, slot), 0)
        < lax.broadcasted_iota(jnp.int32, (slot, slot), 1)
    )
    upper = jnp.where(before, 1.0, 0.0).astype(BF16)
    for m in range(micro):
        ids = lax.broadcasted_iota(jnp.int32, (experts, slot), 0)
        picks = [ids == route_ref[m, c : c + 1, :] for c in range(top_count)]
        named = jnp.where(picks[0] | picks[1], 1.0, 0.0).astype(BF16)
        places = dot(named, upper)
        valid = jnp.where(
            lax.broadcasted_iota(jnp.int32, (1, slot), 1) < len_ref[0, m], 1.0, 0.0
        )
        for c in range(top_count):
            place = jnp.sum(jnp.where(picks[c], places, 0.0), axis=0, keepdims=True)
            info_ref[m, c : c + 1, :] = place + (route_ref[m, c : c + 1, :] * cap).astype(F32)
            info_ref[m, 2 + c : 3 + c, :] = gate_ref[m, c : c + 1, :] * valid
        info_ref[m, 4:5, :] = valid
        info_ref[m, 5:8, :] = jnp.zeros((3, slot), F32)


def plan_routes(lengths, routes, gates, cap, experts):
    micro, _, slot = routes.shape
    return call(
        functools.partial(routes_kernel, cap, experts),
        sds((micro, 8, slot), F32),
        [SM, VM, VM],
        VM,
        flops=1e8,
        nbytes=3e6,
        name="plan_routes",
    )(lengths, routes, gates)


def grad_rows_kernel(cap, me_ref, info_ref, grad_ref, send_ref):
    me = me_ref[0]
    pairs = []
    valid = info_ref[0, 4:5, :]
    for c in range(2):
        gate = info_ref[0, 2 + c : 3 + c, :]
        main = grad_ref[0, pl.ds(main_first(me), LANES), :].astype(F32) * valid * gate
        tail = grad_ref[0, pl.ds(tail_first(me), HALF), :].astype(F32) * valid * gate
        pairs.append(wide_pair(main, tail))
    dispatch(send_ref, pairs, [[info_ref[0, c : c + 1, :]] for c in range(2)], cap)


def gradient_rows(me, info, grads, m, cap, experts):
    return call(
        functools.partial(grad_rows_kernel, cap),
        sds((experts, cap + cap // 2, LANES), BF16),
        [SM, at(info, m), at(grads, m)],
        whole(sds((experts, cap + cap // 2, LANES), BF16)),
        grid=(1,),
        flops=1.5e9,
        nbytes=3e6,
        name=f"gradient_rows_{m}",
    )(me, info, grads)


def stage_shards(shards, scratch, sems, me):
    copies = [
        pltpu.make_async_copy(shard, scratch.at[me ^ j], sems.at[j])
        for j, shard in enumerate(shards)
    ]
    for c in copies:
        c.start()
    return copies


def put_blocks(wide_ref, keep_ref, send_ref, me):
    keep_ref[0] = wide_ref[me]
    keep_ref[1] = wide_ref[me ^ 2]
    send_ref[0] = wide_ref[me ^ 1].astype(BF16)
    send_ref[1] = wide_ref[me ^ 3].astype(BF16)


def distance_tiles(block):
    keys = lax.broadcasted_iota(jnp.int32, (block, block), 0)
    queries = lax.broadcasted_iota(jnp.int32, (block, block), 1)
    return queries - keys, queries - keys + block


def bias_tiles(table_ref, starts, head, block):
    out = []
    for dist in distance_tiles(block):
        tile = jnp.full((block, block), table_ref[head, 0], F32)
        for b in range(1, len(starts)):
            tile = jnp.where(dist >= starts[b], table_ref[head, b], tile)
        out.append(tile)
    return out


def probabilities(k, q, biases, far_bias, seq_len, i, block, scale):
    keys = block * (i + 1)
    s = dot(k, q) * scale
    near = distance_tiles(block)[0]
    pieces = []
    for j in range(i + 1):
        sub = s[block * j : block * (j + 1)]
        if j == i:
            sub = jnp.where(near >= 0, sub + biases[0], NEG_LARGE)
        elif j == i - 1:
            sub = sub + biases[1]
        else:
            sub = sub + far_bias
        pieces.append(sub)
    s = jnp.concatenate(pieces, axis=0) if i else pieces[0]
    s = jnp.where(lax.broadcasted_iota(jnp.int32, (keys, block), 0) < seq_len, s, NEG_LARGE)
    e = jnp.exp(s - jnp.max(s, axis=0, keepdims=True))
    return e / jnp.sum(e, axis=0, keepdims=True)


def forward_kernel(
    starts, parts, micro_idx, me_ref, len_ref, table_ref, s0, s1, s2, s3, g0, g1, g2, g3,
    wq_ref, wo_ref, qkv_ref, att_ref, keep_ref, send_ref, gain_row_ref, gain_col_ref,
    x_s, gain_s, wide_s, sems,
):
    me = me_ref[0]
    waits = stage_shards((s0, s1, s2, s3), x_s, sems.at[0], me)
    waits += stage_shards((g0, g1, g2, g3), gain_s, sems.at[1], me)
    for c in waits:
        c.wait()
    pw, slot = att_ref.shape
    heads = table_ref.shape[0]
    hd = pw // heads
    width = parts * pw
    block = min(LANES, slot)
    for i in range(parts):
        for a in range(2):
            gain_row_ref[a : a + 1, pw * i : pw * (i + 1)] = gain_s[i, a : a + 1, :pw]
        column = jnp.broadcast_to(gain_s[i, 0:1, :], (LANES, GAIN_WIDTH)).T
        gain_col_ref[pw * i : pw * (i + 1), :] = column[:pw]
    x = x_s[...].reshape(width, slot).astype(F32)
    r1 = lax.rsqrt(jnp.sum(x * x, axis=0, keepdims=True) / width + EPSILON)
    gain = jnp.concatenate([gain_col_ref[...]] * (slot // LANES), axis=1)
    n1 = (x * r1 * gain).astype(BF16)
    for c in range(3):
        qkv_ref[c] = dot(wq_ref[c], n1).astype(BF16)
    seq_len = len_ref[0, micro_idx]
    scale = 1.0 / math.sqrt(hd)
    k_all = qkv_ref[1].astype(F32).T.astype(BF16)
    for h in range(heads):
        part = slice(hd * h, hd * (h + 1))
        biases = bias_tiles(table_ref, starts, h, block)
        far = table_ref[h, len(starts) - 1]
        k = k_all[:, part]
        for i in range(slot // block):
            keys = block * (i + 1)
            rows = slice(block * i, block * (i + 1))
            p = probabilities(
                k[:keys], qkv_ref[0, part, rows], biases, far, seq_len, i, block, scale
            ).astype(BF16)
            att_ref[part, rows] = dot(qkv_ref[2, part, :keys], p).astype(BF16)
    wide_s[...] = dot_tn(wo_ref[...], att_ref[...]).reshape(parts, pw, slot)
    put_blocks(wide_s, keep_ref, send_ref, me)


def forward(me, lengths, table, shards, gains, wq, wo, m, starts):
    parts = len(shards)
    pw, slot = shards[0].shape
    width = parts * pw
    return call(
        functools.partial(forward_kernel, starts, parts, m),
        [
            sds((3, pw, slot), BF16),
            sds((pw, slot), BF16),
            sds((2, pw, slot), F32),
            sds((2, pw, slot), BF16),
            sds((2, width), F32),
            sds((width, LANES), F32),
        ],
        [SM, SM, SM] + [ANY] * (2 * parts) + [VM, VM],
        [VM] * 6,
        [
            pltpu.VMEM((parts, pw, slot), BF16),
            pltpu.VMEM((parts,) + gains[0].shape, F32),
            pltpu.VMEM((parts, pw, slot), F32),
            pltpu.SemaphoreType.DMA((2, parts)),
        ],
        flops=6e9,
        nbytes=1e7,
        name=f"forward_{m}",
    )(me, lengths, table, *shards, *gains, wq, wo)


def middle_kernel(
    cap, me_ref, x_ref, keep_ref, got_core_ref, got_x_ref, info_ref, mid_ref, send_ref
):
    me = me_ref[0]
    mid_ref[...] = (
        x_ref[0].astype(F32)
        + keep_ref[0]
        + got_core_ref[0].astype(F32)
        + got_x_ref[...].astype(F32)
    )
    pair = wide_pair(
        mid_ref[pl.ds(main_first(me), LANES), :], mid_ref[pl.ds(tail_first(me), HALF), :]
    )
    dispatch(send_ref, [pair], [[info_ref[0, c : c + 1, :] for c in range(2)]], cap)


def middle(me, x, keep, got_core, got_x, info, m, cap, experts):
    _, pw, slot = x.shape
    outs = [sds((pw, slot), F32), sds((experts, cap + cap // 2, LANES), BF16)]
    return call(
        functools.partial(middle_kernel, cap),
        outs,
        [SM, at(x, m), at(keep, 0), at(got_core, 0), whole(got_x), at(info, m)],
        [whole(o) for o in outs],
        grid=(1,),
        flops=2e9,
        nbytes=3e6,
        name=f"middle_{m}",
    )(me, x, keep, got_core, got_x, info)


def load_rows(scratch, step, spread, cap, parts):
    half = cap // 2
    tiles = []
    for k in range(0, parts, 2):
        mains, tails = [], []
        for i in (k, k + 1):
            ref = scratch.at[i, pl.ds(step * spread, spread)]
            mains.append(ref[:, :cap, :].astype(F32).reshape(spread * cap, LANES))
            tails.append(ref[:, cap:, :].astype(F32).reshape(spread * half, LANES))
        top, bottom = mix_tails(*tails)
        tile = jnp.concatenate(
            [top.reshape(spread, half, LANES), bottom.reshape(spread, half, LANES)], axis=1
        ).reshape(spread * cap, LANES)
        tiles += [mains[0], tile, mains[1]]
    return jnp.concatenate(tiles, axis=1)


def put_rows(wide, scratch, keep_ref, send_ref, me, spread, cap, parts):
    half = cap // 2
    for k in range(0, parts, 2):
        first, tile, second = (
            wide[:, LANES * t : LANES * (t + 1)].reshape(spread, cap, LANES)
            for t in range(3 * k // 2, 3 * k // 2 + 3)
        )
        even, odd = mix_tails(
            tile[:, :half].reshape(spread * half, LANES),
            tile[:, half:].reshape(spread * half, LANES),
        )
        scratch[k, :, :cap, :] = first
        scratch[k, :, cap:, :] = even.reshape(spread, half, LANES)
        scratch[k + 1, :, :cap, :] = second
        scratch[k + 1, :, cap:, :] = odd.reshape(spread, half, LANES)
    put_blocks(scratch, keep_ref, send_ref, me)


def expert_kernel(
    parts, spread, cap, me_ref, m0, m1, m2, m3, d0, d1, d2, d3, win_ref, wdown_ref, gain_ref,
    n2_ref, act_ref, dpre_ref, dy_ref, keep_ref, send_ref, gsum_ref, mid_s, dy_s, blocks, sems,
):
    me = me_ref[0]
    step = pl.program_id(0)
    steps = pl.num_programs(0)

    def copies(when):
        out = []
        part = pl.ds(when * spread, spread)
        for a, (shards, scratch) in enumerate((((m0, m1, m2, m3), mid_s), ((d0, d1, d2, d3), dy_s))):
            for j, shard in enumerate(shards):
                out.append(
                    pltpu.make_async_copy(
                        shard.at[part], scratch.at[me ^ j, part], sems.at[a, j, when]
                    )
                )
        return out

    @pl.when(step == 0)
    def _():
        @pl.loop(0, steps)
        def _(when):
            for c in copies(when):
                c.start()

        gsum_ref[...] = jnp.zeros_like(gsum_ref)

    for c in copies(step):
        c.wait()
    width = win_ref.shape[0]
    mid = load_rows(mid_s, step, spread, cap, parts)
    dy = load_rows(dy_s, step, spread, cap, parts).astype(BF16)
    gain = gain_ref[1:2, :]
    r2 = lax.rsqrt(jnp.sum(mid * mid, axis=1, keepdims=True) / width + EPSILON)
    xr = mid * r2
    n2 = (xr * gain).astype(BF16)
    pre = dot(n2, win_ref[...])
    cdf = 0.5 * (1.0 + lax.erf(pre * (1.0 / math.sqrt(2.0))))
    act_ref[...] = (pre * cdf).astype(BF16)
    slope = cdf + pre * (jnp.exp(-0.5 * pre * pre) * (1.0 / math.sqrt(2.0 * math.pi)))
    dact = dot_nt(dy, wdown_ref[...])
    dpre = (dact * slope).astype(BF16)
    inner = jnp.sum(dpre.astype(F32) * pre, axis=1, keepdims=True)
    dn2 = dot_nt(dpre, win_ref[...])
    n2_ref[...] = n2
    dy_ref[...] = dy
    dpre_ref[...] = dpre
    gsum_ref[0:1, :] += jnp.sum(dn2 * xr, axis=0, keepdims=True)
    drow = r2 * (dn2 * gain) - xr * (r2 * inner * (1.0 / width))
    put_rows(drow, blocks, keep_ref, send_ref, me, spread, cap, parts)


def row_spread(owners, cap):
    best = 1
    for s in range(1, owners + 1):
        if owners % s == 0 and s * cap <= 320:
            best = s
    return best


def row_blocks(spread, chunk):
    return pl.BlockSpec((2, spread, chunk, LANES), lambda i: (0, i, 0, 0))


def expert_main(me, mids, dys, win, wdown, gains, m, cap):
    parts = len(mids)
    owners, chunk, _ = mids[0].shape
    width, hidden = win.shape
    spread = row_spread(owners, cap)
    steps = owners // spread
    total = owners * cap
    by_row = lambda w: pl.BlockSpec((spread * cap, w), lambda i: (i, 0))
    return call(
        functools.partial(expert_kernel, parts, spread, cap),
        [
            sds((total, width), BF16),
            sds((total, hidden), BF16),
            sds((total, hidden), BF16),
            sds((total, width), BF16),
            sds((2, owners, chunk, LANES), F32),
            sds((2, owners, chunk, LANES), BF16),
            sds((8, width), F32),
        ],
        [SM] + [ANY] * (2 * parts) + [whole(win), whole(wdown), whole(gains)],
        [
            by_row(width),
            by_row(hidden),
            by_row(hidden),
            by_row(width),
            row_blocks(spread, chunk),
            row_blocks(spread, chunk),
            whole(sds((8, width), F32)),
        ],
        [
            pltpu.VMEM((parts, owners, chunk, LANES), BF16),
            pltpu.VMEM((parts, owners, chunk, LANES), BF16),
            pltpu.VMEM((parts, spread, chunk, LANES), F32),
            pltpu.SemaphoreType.DMA((2, parts, steps)),
        ],
        grid=(steps,),
        flops=6 * total * width * hidden,
        nbytes=2e7,
        name=f"expert_{m}",
    )(me, *mids, *dys, win, wdown, gains)


def down_kernel(parts, spread, cap, me_ref, act_ref, wdown_ref, keep_ref, send_ref, blocks):
    put_rows(
        dot(act_ref[...], wdown_ref[...]), blocks, keep_ref, send_ref, me_ref[0], spread, cap, parts
    )


def expert_down_rows(me, act, wdown, owners, parts, m, cap):
    total, hidden = act.shape
    width = wdown.shape[1]
    chunk = cap + cap // 2
    spread = row_spread(owners, cap)
    return call(
        functools.partial(down_kernel, parts, spread, cap),
        [
            sds((2, owners, chunk, LANES), F32),
            sds((2, owners, chunk, LANES), BF16),
        ],
        [SM, pl.BlockSpec((spread * cap, hidden), lambda i: (i, 0)), whole(wdown)],
        [row_blocks(spread, chunk)] * 2,
        [pltpu.VMEM((parts, spread, chunk, LANES), F32)],
        grid=(owners // spread,),
        flops=2 * total * width * hidden,
        nbytes=1e7,
        name=f"down_{m}",
    )(me, act, wdown)


def token_sums(rows_ref, dest_rows, cap):
    owners = rows_ref.shape[0]
    half = cap // 2
    tokens = dest_rows[0].shape[1]
    hit = chosen(dest_rows, 0, owners * cap)
    mains = rows_ref[:, :cap, :].reshape(owners * cap, LANES)
    tails = rows_ref[:, cap:, :].reshape(owners * half, LANES)
    split = hit.reshape(owners, cap, tokens)
    low = split[:, :half].reshape(owners * half, tokens)
    high = split[:, half:].reshape(owners * half, tokens)
    return dot_tn(mains, hit), dot_tn(tails, low)[:HALF] + dot_tn(tails, high)[HALF:]


def dmid_kernel(cap, me_ref, rows_ref, info_ref, grad_ref, dmid_ref, low_ref):
    me = me_ref[0]
    main, tail = token_sums(rows_ref, [info_ref[0, c : c + 1, :] for c in range(2)], cap)
    dmid_ref[...] = grad_ref[0].astype(F32) * info_ref[0, 4:5, :]
    dmid_ref[pl.ds(main_first(me), LANES), :] += main
    dmid_ref[pl.ds(tail_first(me), HALF), :] += tail
    low_ref[...] = dmid_ref[...].astype(BF16)


def mid_gradient(me, rows, info, grads, m, cap):
    _, pw, slot = grads.shape
    outs = [sds((pw, slot), F32), sds((pw, slot), BF16)]
    return call(
        functools.partial(dmid_kernel, cap),
        outs,
        [SM, whole(rows), at(info, m), at(grads, m)],
        [whole(o) for o in outs],
        grid=(1,),
        flops=2e9,
        nbytes=3e6,
        name=f"dmid_{m}",
    )(me, rows, info, grads)


def output_kernel(cap, me_ref, rows_ref, info_ref, mid_ref, out_ref):
    me = me_ref[0]
    out_ref[...] = mid_ref[...]
    for c in range(2):
        main, tail = token_sums(rows_ref, [info_ref[0, c : c + 1, :]], cap)
        gate = info_ref[0, 2 + c : 3 + c, :]
        out_ref[pl.ds(main_first(me), LANES), :] += gate * main
        out_ref[pl.ds(tail_first(me), HALF), :] += gate * tail


def block_result(me, rows, info, mid, m, cap):
    return call(
        functools.partial(output_kernel, cap),
        sds(mid.shape, F32),
        [SM, whole(rows), at(info, m), whole(mid)],
        whole(mid),
        grid=(1,),
        flops=2e9,
        nbytes=3e6,
        name=f"output_{m}",
    )(me, rows, info, mid)


def backward_kernel(
    starts, parts, micro_idx, first, last, me_ref, len_ref, table_ref, d0, d1, d2, d3,
    s0, s1, s2, s3, qkv_ref, att_ref, wq_ref, wo_ref, gain_ref, *rest,
):
    if first:
        prior = None
    else:
        prior, rest = rest[:3], rest[3:]
    keep_ref, send_ref, gw_ref, diag_ref, small_ref, *rest = rest
    if last:
        pos_ref, *rest = rest
    dout_s, x_s, wide_s, dqkv_s, sems, pos_s = rest
    me = me_ref[0]
    waits = stage_shards((d0, d1, d2, d3), dout_s, sems.at[0], me)
    waits += stage_shards((s0, s1, s2, s3), x_s, sems.at[1], me)
    for c in waits:
        c.wait()
    pw, slot = att_ref.shape
    heads = table_ref.shape[0]
    hd = pw // heads
    width = parts * pw
    block = min(LANES, slot)
    seq_len = len_ref[0, micro_idx]
    scale = 1.0 / math.sqrt(hd)

    dout = dout_s[...].reshape(width, slot)
    datt = dot(wo_ref[...], dout).astype(BF16)
    go = dot_nt(att_ref[...], dout)

    dqkv_s[...] = jnp.zeros_like(dqkv_s)
    k_all = qkv_ref[1].astype(F32).T.astype(BF16)
    v_all = qkv_ref[2].astype(F32).T.astype(BF16)
    count = len(starts)
    for h in range(heads):
        part = slice(hd * h, hd * (h + 1))
        biases = bias_tiles(table_ref, starts, h, block)
        far = table_ref[h, count - 1]
        k, v = k_all[:, part], v_all[:, part]
        near_sum = jnp.zeros((block, block), F32)
        next_sum = jnp.zeros((block, block), F32)
        far_sum = jnp.zeros((1, block), F32)
        for i in range(slot // block):
            keys = block * (i + 1)
            rows = slice(block * i, block * (i + 1))
            q, da = qkv_ref[0, part, rows], datt[part, rows]
            p = probabilities(k[:keys], q, biases, far, seq_len, i, block, scale)
            dp = dot(v[:keys], da)
            delta = jnp.sum(dp * p, axis=0, keepdims=True)
            ds = (p * (dp - delta)).astype(BF16)
            dqkv_s[2, part, :keys] += dot_nt(da, p.astype(BF16))
            dqkv_s[1, part, :keys] += dot_nt(q, ds)
            dqkv_s[0, part, rows] = dot(qkv_ref[1, part, :keys], ds)
            wide = ds.astype(F32)
            near_sum = near_sum + wide[block * i :]
            if i >= 1:
                next_sum = next_sum + wide[block * (i - 1) : block * i]
            if i >= 2:
                far_sum = far_sum + jnp.sum(wide[: block * (i - 1)], axis=0, keepdims=True)
        if prior is not None:
            near_sum = near_sum + prior[1][2 * h]
            next_sum = next_sum + prior[1][2 * h + 1]
            far_sum = far_sum + prior[2][:1, LANES * (h + 1) : LANES * (h + 1) + block]
        if last:
            tiles = list(zip(distance_tiles(block), (near_sum, next_sum)))
            for b in range(count):
                row = far_sum if b + 1 == count else jnp.zeros((1, block), F32)
                for dist, total in tiles:
                    hit = dist >= starts[b]
                    if b + 1 < count:
                        hit = hit & (dist < starts[b + 1])
                    row = row + jnp.sum(jnp.where(hit, total, 0.0), axis=0, keepdims=True)
                pos_s[h, b : b + 1, :] = row
        else:
            diag_ref[2 * h] = near_sum
            diag_ref[2 * h + 1] = next_sum
            small_ref[:1, LANES * (h + 1) : LANES * (h + 1) + block] = far_sum

    gain = jnp.concatenate([gain_ref[...]] * (slot // LANES), axis=1)
    x = x_s[...].reshape(width, slot).astype(F32)
    r1 = lax.rsqrt(jnp.sum(x * x, axis=0, keepdims=True) / width + EPSILON)
    xr = x * r1
    n1 = (xr * gain).astype(BF16)
    inner = jnp.zeros((1, slot), F32)
    dn1 = jnp.zeros((width, slot), F32)
    for c in range(3):
        d = dqkv_s[c]
        if c < 2:
            d = d * scale
        low = d.astype(BF16)
        inner = inner + jnp.sum(low.astype(F32) * qkv_ref[c].astype(F32), axis=0, keepdims=True)
        dn1 = dn1 + dot_tn(wq_ref[c], low)
        gq = dot_nt(low, n1)
        if prior is not None:
            gq = gq + prior[0][pw * c : pw * (c + 1)]
        gw_ref[pw * c : pw * (c + 1), :] = gq.astype(gw_ref.dtype)
    if prior is not None:
        go = go + prior[0][3 * pw :]
    gw_ref[3 * pw :, :] = go.astype(gw_ref.dtype)
    gain_sum = jnp.sum(dn1 * xr, axis=1, keepdims=True)
    if prior is not None:
        gain_sum = gain_sum + prior[2][:, 0:1]
    small_ref[:, 0:1] = gain_sum
    if last:
        for h in range(heads):
            pos_ref[:, h : h + 1] = jnp.sum(pos_s[h], axis=1, keepdims=True)
    wide_s[...] = (r1 * (dn1 * gain) - xr * (r1 * inner * (1.0 / width))).reshape(
        parts, pw, slot
    )
    put_blocks(wide_s, keep_ref, send_ref, me)


def backward(
    me, lengths, table, dshards, xshards, qkv, att, wq, wo, gain, prior, m, last, starts
):
    parts = len(dshards)
    pw, slot = att.shape
    width = parts * pw
    block = min(LANES, slot)
    heads, buckets = table.shape
    outs = [
        sds((2, pw, slot), F32),
        sds((2, pw, slot), BF16),
        sds((4 * pw, width), BF16 if last else F32),
        sds((2 * heads, block, block), F32),
        sds((width, LANES * (heads + 1)), F32),
    ]
    if last:
        outs.append(sds((buckets, LANES), F32))
    extra = () if prior is None else tuple(prior)
    return call(
        functools.partial(backward_kernel, starts, parts, m, prior is None, last),
        outs,
        [SM, SM, SM] + [ANY] * (2 * parts) + [VM] * (5 + len(extra)),
        [VM] * len(outs),
        [
            pltpu.VMEM((parts, pw, slot), BF16),
            pltpu.VMEM((parts, pw, slot), BF16),
            pltpu.VMEM((parts, pw, slot), F32),
            pltpu.VMEM((3, pw, slot), F32),
            pltpu.SemaphoreType.DMA((2, parts)),
            pltpu.VMEM((heads, buckets, block), F32),
        ],
        flops=8e9,
        nbytes=1.5e7,
        name=f"backward_{m}",
    )(me, lengths, table, *dshards, *xshards, qkv, att, wq, wo, gain, *extra)


def swap(value, flip):
    count = lax.axis_size("tensor")
    return lax.ppermute(value, "tensor", [(i, i ^ flip) for i in range(count)])


def gather_shards(own):
    with jax.named_scope("x"):
        across = swap(own, 2)
    with jax.named_scope("c"):
        beside = swap(own, 1)
    with jax.named_scope("d"):
        far = swap(across, 1)
    return (own, beside, across, far)


def exchange(value):
    return lax.all_to_all(value, "expert", split_axis=0, concat_axis=0, tiled=True)


def reduce_blocks(keep, send):
    with jax.named_scope("c"):
        got_core = swap(send, 1)
    with jax.named_scope("a"):
        onward = (keep[1] + got_core[1].astype(F32)).astype(BF16)
    with jax.named_scope("x"):
        return got_core, swap(onward, 2)


def reduce_rows(keep, send):
    got_core, got_x = reduce_blocks(keep, send)
    with jax.named_scope("b"):
        return (keep[0] + got_core[0].astype(F32) + got_x.astype(F32)).astype(BF16)


def pad_rows(value, multiple):
    short = -value.shape[0] % multiple
    return jnp.pad(value, ((0, short), (0, 0))) if short else value


def local(
    block_input,
    norm1_gain,
    qkv_weight,
    out_weight,
    pos_table,
    norm2_gain,
    expert_in,
    expert_down,
    lengths,
    routes,
    gate_weights,
    output_grad,
):
    micro_count, slot_len, pw = block_input.shape
    parts = lax.axis_size("tensor")
    owners = lax.axis_size("expert")
    experts = expert_in.shape[0] * owners
    assert parts == 4 and expert_in.shape[0] == 1 and pw == LANES + HALF
    width = parts * pw
    top_count = routes.shape[2]
    need = max(2, 5 * slot_len * top_count // (4 * experts))
    cap = -(-need // 32) * 32
    bucket_count, heads = pos_table.shape
    starts = bucket_starts(bucket_count, MAX_DIST)
    me = lax.axis_index("tensor").astype(jnp.int32)[None]
    scope = jax.named_scope

    x = jnp.swapaxes(block_input, 1, 2)
    grads = jnp.swapaxes(output_grad, 1, 2)
    wq = jnp.swapaxes(qkv_weight, 1, 2)
    wo = out_weight
    win, wdown = expert_in[0], expert_down[0]
    table = pos_table.T
    lens = lengths.T
    gains = jnp.pad(jnp.stack([norm1_gain, norm2_gain]), ((0, 6), (0, GAIN_WIDTH - pw)))

    xshards = []
    for m in range(micro_count):
        with scope(f"px_{m}"):
            xshards.append(gather_shards(x[m]))
        if m == 0:
            with scope("pg"):
                gshards = gather_shards(gains)
    info = plan_routes(
        lens, jnp.swapaxes(routes, 1, 2), jnp.swapaxes(gate_weights, 1, 2), cap, experts
    )
    dys = []
    for m in range(micro_count):
        sent = gradient_rows(me, info, grads, m, cap, experts)
        with scope(f"dyA_{m}"):
            sent = exchange(sent)
        with scope(f"dyX_{m}"):
            dys.append(gather_shards(sent))

    fwd, mids, rows_in = [], [], []
    for m in range(micro_count):
        qkv, att, keep, send, gain_row, gain_col = forward(
            me, lens, table, xshards[m], gshards, wq, wo, m, starts
        )
        with scope(f"rs_{m}"):
            got_core, got_x = reduce_blocks(keep, send)
        mid, sent = middle(me, x, keep, got_core, got_x, info, m, cap, experts)
        fwd.append((qkv, att, gain_row, gain_col))
        mids.append(mid)
        with scope(f"nA_{m}"):
            sent = exchange(sent)
        with scope(f"nX_{m}"):
            rows_in.append(gather_shards(sent))

    expert_out, dmids = [], []
    for m in range(micro_count):
        n2, act, dpre, dy, keep, send, gsum = expert_main(
            me, rows_in[m], dys[m], win, wdown, fwd[m][2], m, cap
        )
        expert_out.append((n2, act, dpre, dy, gsum))
        with scope(f"es_{m}"):
            back = reduce_rows(keep, send)
        with scope(f"eA_{m}"):
            back = exchange(back)
        dmids.append(mid_gradient(me, back, info, grads, m, cap))

    prior, terms = None, []
    for m in range(micro_count):
        dmid, low = dmids[m]
        last = m == micro_count - 1
        qkv, att, _, gain_col = fwd[m]
        with scope(f"dX_{m}"):
            dshards = gather_shards(low)
        keep, send, gw, diag, small, *pos = backward(
            me, lens, table, dshards, xshards[m], qkv, att, wq, wo, gain_col, prior, m, last, starts
        )
        prior = (gw, diag, small)
        with scope(f"bs_{m}"):
            terms.append((dmid, keep) + reduce_blocks(keep, send))

    outputs = []
    for m in range(micro_count):
        keep, send = expert_down_rows(me, expert_out[m][1], wdown, owners, parts, m, cap)
        with scope(f"ys_{m}"):
            back = reduce_rows(keep, send)
        with scope(f"yA_{m}"):
            back = exchange(back)
        outputs.append(block_result(me, back, info, mids[m], m, cap))

    with scope("wgrads"):
        grad_in = sum(dot_tn(n2, dpre) for n2, _, dpre, _, _ in expert_out)
        grad_down = sum(dot_tn(act, dy) for _, act, _, dy, _ in expert_out)

    with scope("tiny"):
        sums = jnp.stack([small[:, 0], sum(e[4][0] for e in expert_out)])
        sums = sums + swap(sums, 2)
        sums = sums + swap(sums, 1)
        own = lax.dynamic_slice_in_dim(sums, me[0] * pw, pw, 1)
        flat = jnp.concatenate([own.reshape(-1), pos[0][:, :heads].reshape(-1)])
        flat = jnp.pad(flat, (0, width - flat.shape[0]))[None]
        high = flat.astype(BF16)
        rest = (flat - high.astype(F32)).astype(BF16)
        tiny = jnp.pad(jnp.concatenate([high, rest], axis=0), ((0, 6), (0, 0)))

    gw_rows = gw.shape[0]
    with scope("wA"):
        got = exchange(pad_rows(gw, 8 * owners).reshape(owners, -1, width))
    with scope("wsum"):
        share = jnp.sum(got.astype(F32), axis=0).astype(BF16)
        sent = jnp.concatenate([share, tiny], axis=0)
        sent = jnp.broadcast_to(sent[None], (owners,) + sent.shape)
    with scope("wB"):
        got = exchange(sent)
    with scope("wend"):
        n = share.shape[0]
        gw_all = got[:, :n].reshape(-1, width)[:gw_rows].astype(F32)
        tiny_all = jnp.sum(got[:, n:].astype(F32), axis=0)
        flat = tiny_all[0] + tiny_all[1]

    with scope("final"):
        input_grad = jnp.stack(
            [
                dmid + keep[0] + got_core[0].astype(F32) + got_x.astype(F32)
                for dmid, keep, got_core, got_x in terms
            ]
        )
    return (
        jnp.swapaxes(jnp.stack(outputs), 1, 2),
        jnp.swapaxes(input_grad, 1, 2),
        flat[:pw],
        jnp.swapaxes(gw_all[: 3 * pw].reshape(3, pw, width), 1, 2),
        gw_all[3 * pw :],
        flat[2 * pw : 2 * pw + bucket_count * heads].reshape(bucket_count, heads),
        flat[pw : 2 * pw],
        grad_in[None],
        grad_down[None],
    )


def solution(mesh):
    in_specs = (
        P(None, "expert", "tensor"),
        P("tensor"),
        P(None, None, "tensor"),
        P("tensor", None),
        P(None, "tensor"),
        P("tensor"),
        P("expert", None, "tensor"),
        P("expert", "tensor", None),
        P(None, "expert"),
        P(None, "expert", None),
        P(None, "expert", None),
        P(None, "expert", "tensor"),
    )
    out_specs = (
        P(None, "expert", "tensor"),
        P(None, "expert", "tensor"),
        P("tensor"),
        P(None, None, "tensor"),
        P("tensor", None),
        P(None, "tensor"),
        P("tensor"),
        P("expert", None, "tensor"),
        P("expert", "tensor", None),
    )
    return jax.shard_map(local, mesh=mesh, in_specs=in_specs, out_specs=out_specs, check_vma=False)
```
